128 devices in a mesh: seg: 128 (over x, y, z, core).
Axes of the slice: x: 4, y: 4, z: 4, core: 2. Of those that a mesh axis runs over, the one named last changes fastest.
Arguments:
- tokens: bfloat16 [32768, 3584], P('seg'), may hold values from -6 to 6
- memory: bfloat16 [64, 3584], replicated, may hold values from -6 to 6
- norm_gain: float32 [3584], replicated, may hold values from 0.5 to 2
- post_gain: float32 [3584], replicated, may hold values from 0.5 to 2
- query_weight: bfloat16 [3584, 2048], P('seg'), may hold values from -0.09375 to 0.09375
- key_matrix: bfloat16 [3584, 1024], replicated, may hold values from -0.09375 to 0.09375
- value_matrix: bfloat16 [3584, 1024], replicated, may hold values from -0.09375 to 0.09375
- output_weight: bfloat16 [2048, 3584], P('seg'), may hold values from -0.125 to 0.125
- segment_weight: float32 [128], P('seg'), may hold values from 0.1 to 4
Outputs:
- token_out: bfloat16 [32768, 3584], P('seg')
- memory_out: bfloat16 [8192, 3584], P('seg')
- changes: float32 [3], replicated
The draws below stay inside these ranges and needn't reach their ends.
All inputs are finite; a program needn't handle non-finite values.
Results may differ from the reference program's by a relative error of at most 0.014.
Values may be sent and summed in bfloat16 or wider, within the bound.
No kernel may reach another device: no remote copies, remote signals or barrier semaphores. Data moves between devices by JAX's collectives and lax.ppermute only.
A program may use at most 192 MiB of HBM per device.

```python
import math
import jax
import jax.numpy as jnp
from jax import lax

MODEL_WIDTH = 3584
HEAD_WIDTH = 256
HQ = 8
KEY_VALUE_HEADS = 4
MEM = 64
ITERS = 3
TOK_DEV = 256
SEGMENTS = 128
N_SEG = 128


def draw_segment_weight(key, part):
    ramp = jnp.arange(SEGMENTS).astype(jnp.float32) / max(SEGMENTS - 1, 1)
    level = jax.random.uniform(key, (SEGMENTS,), jnp.float32, 0.0, 1.0)
    return 0.1 + 0.3 * ramp + 3.6 * jnp.power(level, 8.0)


def level_of(stream_key, dims, split, low, high):
    factor_of = 1.0
    for dim, blocks in split:
        draws = jax.random.uniform(jax.random.fold_in(jax.random.fold_in(stream_key, 6), dim), (blocks,), jnp.float32, low / len(split), high / len(split))
        factor_of = factor_of * jnp.repeat(jnp.exp(draws), dims[dim] // blocks).reshape((-1,) + (1,) * (len(dims) - 1 - dim))
    return factor_of


def bell_draw(key, shape, spread, limit, shards=(), dtype=jnp.bfloat16):
    result = jax.random.normal(key, shape, jnp.float32) * spread
    if len(shards) > 0:
        result = level_of(key, shape, shards, -0.22, 0.18) * result
    return jnp.clip(result, min=-limit, max=limit).astype(dtype)


def setup_inputs(seed: int = 0) -> dict:
    key_list = jax.random.split(jax.random.key(seed), 10)
    return {
        "tokens": bell_draw(key_list[0], (SEGMENTS * TOK_DEV, MODEL_WIDTH), 1.0, 6.0, ((0, 128),)),
        "memory": bell_draw(key_list[1], (MEM, MODEL_WIDTH), 1.0, 6.0),
        "norm_gain": jnp.clip(jnp.exp(jax.random.uniform(key_list[2], (MODEL_WIDTH,), jnp.float32, math.log(0.5), math.log(2.0))), 0.5, 2.0),
        "post_gain": jnp.clip(jnp.exp(jax.random.uniform(key_list[3], (MODEL_WIDTH,), jnp.float32, math.log(0.5), math.log(2.0))), 0.5, 2.0),
        "query_weight": bell_draw(key_list[4], (MODEL_WIDTH, HQ * HEAD_WIDTH), MODEL_WIDTH ** -0.5, 0.09375, ((0, 128),)),
        "key_matrix": bell_draw(key_list[5], (MODEL_WIDTH, KEY_VALUE_HEADS * HEAD_WIDTH), MODEL_WIDTH ** -0.5, 0.09375),
        "value_matrix": bell_draw(key_list[6], (MODEL_WIDTH, KEY_VALUE_HEADS * HEAD_WIDTH), MODEL_WIDTH ** -0.5, 0.09375),
        "output_weight": bell_draw(key_list[7], (HQ * HEAD_WIDTH, MODEL_WIDTH), (HQ * HEAD_WIDTH) ** -0.5, 0.125, ((0, 128),)),
        "segment_weight": draw_segment_weight(jax.random.fold_in(key_list[9], 71), 0),
    }


eps = 1e-06

def prenorm(rows, gain):
    rows = rows.astype(jnp.float32)
    mean_sq = lax.optimization_barrier(jnp.mean(rows * rows, axis=-1, keepdims=True))
    return (rows / jnp.sqrt(mean_sq + eps) * gain).astype(jnp.bfloat16)

def attend(query_vectors, key_vectors, value_vectors, allowed):
    element_count = query_vectors.shape[0]
    feature_width = key_vectors.shape[0]
    query_heads_split = query_vectors.reshape(element_count, KEY_VALUE_HEADS, 2, HEAD_WIDTH).astype(jnp.float32)
    key_heads_split = key_vectors.reshape(feature_width, KEY_VALUE_HEADS, HEAD_WIDTH).astype(jnp.float32)
    value_heads_split = value_vectors.reshape(feature_width, KEY_VALUE_HEADS, HEAD_WIDTH).astype(jnp.float32)
    score = jnp.einsum('rgjd,kgd->gjrk', query_heads_split, key_heads_split)
    expo = jnp.where(allowed[None, None], jnp.exp(score), 0.0)
    denom = lax.optimization_barrier(jnp.sum(expo, axis=-1))
    weights = expo.astype(jnp.bfloat16).astype(jnp.float32)
    numer = jnp.einsum('gjrk,kgd->rgjd', weights, value_heads_split)
    denom = jnp.transpose(denom, (2, 0, 1))
    attn = numer / denom[:, :, :, None]
    return attn.reshape(element_count, HQ * HEAD_WIDTH).astype(jnp.bfloat16)

def finish(inputs, attn, output_weight, post_gain):
    proj = jnp.dot(attn, output_weight, preferred_element_type=jnp.float32)
    mean_sq = lax.optimization_barrier(jnp.mean(proj * proj, axis=-1, keepdims=True))
    return (inputs.astype(jnp.float32) + proj / jnp.sqrt(mean_sq + eps) * post_gain).astype(jnp.bfloat16)

def project(normed, weight):
    return jnp.dot(normed, weight, preferred_element_type=jnp.float32)

def reference(tokens, memory, norm_gain, post_gain, query_weight, key_matrix, value_matrix, output_weight, segment_weight):
    segs = N_SEG
    scale = 1.0 / HEAD_WIDTH ** 0.5
    seg_tokens = tokens.reshape(segs, TOK_DEV, MODEL_WIDTH)
    write_norm = prenorm(memory, norm_gain)
    write_q = (project(write_norm, query_weight) * scale).astype(jnp.bfloat16)
    write_k = project(write_norm, key_matrix).astype(jnp.bfloat16)
    write_v = project(write_norm, value_matrix).astype(jnp.bfloat16)

    def token_keys(rows):
        normed = prenorm(rows, norm_gain)
        return (project(normed, key_matrix).astype(jnp.bfloat16), project(normed, value_matrix).astype(jnp.bfloat16))
    tok_k, tok_v = lax.map(token_keys, seg_tokens)
    write_mask = jnp.concatenate([jnp.ones((MEM, MEM + TOK_DEV), bool), jnp.tril(jnp.ones((MEM, MEM), bool))], axis=1)

    def write_pass(items):
        read, keys_t, values_t = items
        normed = prenorm(read, norm_gain)
        read_k = project(normed, key_matrix).astype(jnp.bfloat16)
        read_v = project(normed, value_matrix).astype(jnp.bfloat16)
        key_vectors = jnp.concatenate([read_k, keys_t, write_k], axis=0)
        value_vectors = jnp.concatenate([read_v, values_t, write_v], axis=0)
        attn = attend(write_q, key_vectors, value_vectors, write_mask)
        return finish(memory, attn, output_weight, post_gain)
    read_all = jnp.broadcast_to(memory[None], (segs, MEM, MODEL_WIDTH))
    previous = read_all
    changes = []
    newest = previous
    read_used = read_all
    for step in range(ITERS):
        read_used = read_all
        newest = lax.map(write_pass, (read_all, tok_k, tok_v))
        diff = newest.astype(jnp.float32) - previous.astype(jnp.float32)
        per_segment = lax.optimization_barrier(jnp.sum(diff * diff, axis=(1, 2))) * segment_weight
        changes.append(jnp.sqrt(jnp.sum(per_segment) / (segs * MEM * MODEL_WIDTH) + eps))
        previous = newest
        read_all = jnp.concatenate([memory[None], newest[:-1]], axis=0)
    token_mask = jnp.concatenate([jnp.ones((TOK_DEV, MEM), bool), jnp.tril(jnp.ones((TOK_DEV, TOK_DEV), bool))], axis=1)

    def token_pass(items):
        rows, read, keys_t, values_t = items
        normed = prenorm(rows, norm_gain)
        query_vectors = (project(normed, query_weight) * scale).astype(jnp.bfloat16)
        read_norm = prenorm(read, norm_gain)
        read_k = project(read_norm, key_matrix).astype(jnp.bfloat16)
        read_v = project(read_norm, value_matrix).astype(jnp.bfloat16)
        key_vectors = jnp.concatenate([read_k, keys_t], axis=0)
        value_vectors = jnp.concatenate([read_v, values_t], axis=0)
        attn = attend(query_vectors, key_vectors, value_vectors, token_mask)
        return finish(rows, attn, output_weight, post_gain)
    token_out = lax.map(token_pass, (seg_tokens, read_used, tok_k, tok_v))
    return (token_out.reshape(segs * TOK_DEV, MODEL_WIDTH), newest.reshape(segs * MEM, MODEL_WIDTH), jnp.stack(changes).astype(jnp.float32))
```

```python
import functools

import jax
import jax.numpy as jnp
from jax import lax
from jax.experimental import pallas as pl
from jax.experimental.pallas import tpu as pltpu
from jax.sharding import Mesh
from jax.sharding import PartitionSpec as P

HEAD = 256
GROUPS = 4
PAIR = 2 * HEAD
ITERS = 3
WIDTH = 3584
MEM = 64
TOK = 256
ROWS = TOK + MEM
CHUNKS = WIDTH // PAIR
QROWS = 28
QPAD = 32
OROWS = 16
DEVICES = 128
SEG = ("seg_0", "seg_1", "seg_2", "seg_3")
VMEM_BYTES = 60 * 1024 * 1024

eps = 1e-06


def from_behind(block, axis, distance):
    devices = range(lax.axis_size(axis))
    route = [(i - distance, i) for i in devices if i - distance in devices]
    return lax.ppermute(block, axis, route)


def prenorm(rows, gain):
    rows = rows.astype(jnp.float32)
    mean_sq = jnp.mean(rows * rows, axis=-1, keepdims=True)
    return (rows / jnp.sqrt(mean_sq + eps) * gain).astype(jnp.bfloat16)


def dot(a, b):
    return jnp.dot(a, b, preferred_element_type=jnp.float32)


def attend(q, keys, values, row0):
    rows = q.shape[0]
    both = jnp.concatenate([q[:, :HEAD], q[:, HEAD:]], axis=0)
    score = lax.dot_general(
        both, keys, (((1,), (1,)), ((), ())), preferred_element_type=jnp.float32
    )
    row = lax.broadcasted_iota(jnp.int32, score.shape, 0)
    row = jnp.where(row >= rows, row - rows, row) + row0
    col = lax.broadcasted_iota(jnp.int32, score.shape, 1)
    expo = jnp.where(col - MEM <= row, jnp.exp(score), 0.0)
    denom = jnp.sum(expo, axis=-1, keepdims=True)
    numer = dot(expo.astype(jnp.bfloat16), values)
    attn = (numer / denom).astype(jnp.bfloat16)
    return jnp.concatenate([attn[:rows], attn[rows:]], axis=1)


def out_copy(gathered, buf, sem, b):
    first = GROUPS * QPAD + b * OROWS
    return pltpu.make_async_copy(
        gathered.at[:, pl.ds(first, OROWS), :], buf.at[b], sem.at[b]
    )


def project_out(attn_ref, gathered, wobuf, wosem, proj_ref):
    attn = jnp.concatenate([attn_ref[g] for g in range(GROUPS)], axis=1)
    rows = attn.shape[0]

    def block(b, total):
        out_copy(gathered, wobuf, wosem, b).wait()
        proj = dot(attn, wobuf[b].reshape(DEVICES * OROWS, PAIR))
        proj_ref[b] = proj
        return total + jnp.sum(proj * proj, axis=-1, keepdims=True)

    return lax.fori_loop(0, CHUNKS, block, jnp.zeros((rows, 1), jnp.float32))


def finish_rows(proj_ref, start, count, total, residual_ref, gain_ref, out_ref):
    root = jnp.sqrt(total[start : start + count] * (1.0 / WIDTH) + eps)
    for b in range(CHUNKS):
        cols = slice(b * PAIR, (b + 1) * PAIR)
        proj = proj_ref[b, start : start + count, :]
        out = residual_ref[:, cols].astype(jnp.float32) + proj / root * gain_ref[:, cols]
        out_ref[:, cols] = out.astype(jnp.bfloat16)


def squared_change(new_ref, old_ref):
    total = jnp.zeros((MEM, PAIR), jnp.float32)
    for b in range(CHUNKS):
        cols = slice(b * PAIR, (b + 1) * PAIR)
        diff = new_ref[:, cols].astype(jnp.float32) - old_ref[:, cols].astype(jnp.float32)
        total = total + diff * diff
    return jnp.full((8, 128), jnp.sum(total), jnp.float32)


def first_kernel(
    normed_ref, k_ref, v_ref, memory_ref, post_ref, gathered,
    q_ref, new_ref, sq_ref,
    wqbuf, wobuf, attn_ref, proj_ref, wqsem, wosem,
):
    def q_copy(g):
        return pltpu.make_async_copy(
            gathered.at[:, pl.ds(g * QPAD, QPAD), :], wqbuf.at[g], wqsem.at[g]
        )

    for g in range(GROUPS):
        q_copy(g).start()
    for b in range(CHUNKS):
        out_copy(gathered, wobuf, wosem, b).start()

    def group(g, _):
        q_copy(g).wait()
        acc = dot(normed_ref[...], wqbuf[g].reshape(DEVICES * QPAD, PAIR))
        q = (acc * (1.0 / HEAD**0.5)).astype(jnp.bfloat16)
        q_ref[g] = q
        keys = k_ref[g]
        values = v_ref[g]
        keys = jnp.concatenate([keys[TOK:], keys], axis=0)
        values = jnp.concatenate([values[TOK:], values], axis=0)
        attn_ref[g] = attend(q[TOK:], keys, values, TOK)
        return 0

    lax.fori_loop(0, GROUPS, group, 0)
    total = project_out(attn_ref, gathered, wobuf, wosem, proj_ref)
    finish_rows(proj_ref, 0, MEM, total, memory_ref, post_ref, new_ref)
    sq_ref[...] = squared_change(new_ref, memory_ref)


def step_kernel(
    last, first_ref, shifted_ref, previous_ref, memory_ref, tokens_ref, q_ref, k_ref, v_ref,
    gain_ref, post_ref, key_matrix, value_matrix, gathered, *rest,
):
    if last:
        tok_ref, new_ref, sq_ref = rest[:3]
        rest = rest[3:]
    else:
        new_ref, sq_ref = rest[:2]
        rest = rest[2:]
    wkbuf, wvbuf, wobuf, normed_ref, kacc_ref, vacc_ref, attn_ref, proj_ref, ksem, vsem, wosem = rest

    def k_copy(i):
        return pltpu.make_async_copy(
            key_matrix.at[pl.ds(i * PAIR, PAIR), :], wkbuf.at[i], ksem.at[i]
        )

    def v_copy(i):
        return pltpu.make_async_copy(
            value_matrix.at[pl.ds(i * PAIR, PAIR), :], wvbuf.at[i], vsem.at[i]
        )

    for i in range(CHUNKS):
        k_copy(i).start()
        v_copy(i).start()
    for b in range(CHUNKS):
        out_copy(gathered, wobuf, wosem, b).start()

    at_start = first_ref[0] == 1

    def read_rows(i):
        cols = slice(i * PAIR, (i + 1) * PAIR)
        return jnp.where(at_start, memory_ref[:, cols], shifted_ref[:, cols]).astype(jnp.float32)

    total = jnp.zeros((MEM, 1), jnp.float32)
    for i in range(CHUNKS):
        rows = read_rows(i)
        total = total + jnp.sum(rows * rows, axis=-1, keepdims=True)
    root = jnp.sqrt(total * (1.0 / WIDTH) + eps)
    for i in range(CHUNKS):
        cols = slice(i * PAIR, (i + 1) * PAIR)
        normed_ref[i] = (read_rows(i) / root * gain_ref[:, cols]).astype(jnp.bfloat16)
    kacc_ref[...] = jnp.zeros_like(kacc_ref)
    vacc_ref[...] = jnp.zeros_like(vacc_ref)

    def chunk(i, _):
        k_copy(i).wait()
        v_copy(i).wait()
        rows = normed_ref[i]
        kacc_ref[...] += dot(rows, wkbuf[i])
        vacc_ref[...] += dot(rows, wvbuf[i])
        return 0

    lax.fori_loop(0, CHUNKS, chunk, 0)
    row0 = 0 if last else TOK
    for g in range(GROUPS):
        cols = slice(g * HEAD, (g + 1) * HEAD)
        keys = jnp.concatenate([kacc_ref[:, cols].astype(jnp.bfloat16), k_ref[g]], axis=0)
        values = jnp.concatenate([vacc_ref[:, cols].astype(jnp.bfloat16), v_ref[g]], axis=0)
        attn_ref[g] = attend(q_ref[g, row0:, :], keys, values, row0)
    total = project_out(attn_ref, gathered, wobuf, wosem, proj_ref)
    start = 0
    if last:
        finish_rows(proj_ref, 0, TOK, total, tokens_ref, post_ref, tok_ref)
        start = TOK
    finish_rows(proj_ref, start, MEM, total, memory_ref, post_ref, new_ref)
    sq_ref[...] = squared_change(new_ref, previous_ref)


def whole():
    return pl.BlockSpec(memory_space=pltpu.VMEM)


def in_hbm():
    return pl.BlockSpec(memory_space=pl.ANY)


def buffers(*shapes):
    return [pltpu.VMEM(shape, dtype) for shape, dtype in shapes]


OUT_BUFFER = ((CHUNKS, DEVICES, OROWS, PAIR), jnp.bfloat16)


def first_step(normed, k, v, memory, post_gain, gathered):
    return pl.pallas_call(
        first_kernel,
        name="first_step",
        out_shape=(
            jax.ShapeDtypeStruct((GROUPS, ROWS, PAIR), jnp.bfloat16),
            jax.ShapeDtypeStruct((MEM, WIDTH), jnp.bfloat16),
            jax.ShapeDtypeStruct((8, 128), jnp.float32),
        ),
        in_specs=[whole()] * 5 + [in_hbm()],
        out_specs=(whole(), whole(), whole()),
        scratch_shapes=buffers(
            ((GROUPS, DEVICES, QPAD, PAIR), jnp.bfloat16),
            OUT_BUFFER,
            ((GROUPS, MEM, PAIR), jnp.bfloat16),
            ((CHUNKS, MEM, PAIR), jnp.float32),
        )
        + [pltpu.SemaphoreType.DMA((GROUPS,)), pltpu.SemaphoreType.DMA((CHUNKS,))],
        compiler_params=pltpu.CompilerParams(vmem_limit_bytes=VMEM_BYTES),
    )(normed, k, v, memory, post_gain, gathered)


def later_step(
    last, first, shifted, previous, memory, tokens, q, k, v, gain, post_gain,
    key_matrix, value_matrix, gathered,
):
    rows = ROWS if last else MEM
    out_shape = [
        jax.ShapeDtypeStruct((MEM, WIDTH), jnp.bfloat16),
        jax.ShapeDtypeStruct((8, 128), jnp.float32),
    ]
    if last:
        out_shape = [jax.ShapeDtypeStruct((TOK, WIDTH), jnp.bfloat16)] + out_shape
    return pl.pallas_call(
        functools.partial(step_kernel, last),
        name="last_step" if last else "middle_step",
        out_shape=tuple(out_shape),
        in_specs=[pl.BlockSpec(memory_space=pltpu.SMEM)]
        + [whole()] * 3
        + [whole() if last else in_hbm()]
        + [whole()] * 5
        + [in_hbm()] * 3,
        out_specs=tuple(whole() for _ in out_shape),
        scratch_shapes=buffers(
            ((CHUNKS, PAIR, GROUPS * HEAD), jnp.bfloat16),
            ((CHUNKS, PAIR, GROUPS * HEAD), jnp.bfloat16),
            OUT_BUFFER,
            ((CHUNKS, MEM, PAIR), jnp.bfloat16),
            ((MEM, GROUPS * HEAD), jnp.float32),
            ((MEM, GROUPS * HEAD), jnp.float32),
            ((GROUPS, rows, PAIR), jnp.bfloat16),
            ((CHUNKS, rows, PAIR), jnp.float32),
        )
        + [pltpu.SemaphoreType.DMA((CHUNKS,)) for _ in range(3)],
        compiler_params=pltpu.CompilerParams(vmem_limit_bytes=VMEM_BYTES),
    )(first, shifted, previous, memory, tokens, q, k, v, gain, post_gain,
      key_matrix, value_matrix, gathered)


def by_head(x):
    return jnp.transpose(x.reshape(x.shape[0], GROUPS, HEAD), (1, 0, 2))


def shards(
    tokens,
    memory,
    norm_gain,
    post_gain,
    query_weight,
    key_matrix,
    value_matrix,
    output_weight,
    segment_weight,
):
    query_blocks = jnp.pad(query_weight, ((0, QPAD - QROWS), (0, 0)))
    query_blocks = jnp.transpose(query_blocks.reshape(QPAD, GROUPS, PAIR), (1, 0, 2))
    output_blocks = jnp.transpose(output_weight.reshape(OROWS, CHUNKS, PAIR), (1, 0, 2))
    mine = jnp.concatenate(
        [query_blocks.reshape(GROUPS * QPAD, PAIR), output_blocks.reshape(CHUNKS * OROWS, PAIR)],
        axis=0,
    )
    gathered = lax.all_gather(mine, SEG, axis=0, tiled=False)
    inputs = jnp.concatenate([tokens, memory], axis=0)
    normed = prenorm(inputs, norm_gain)
    local_k = by_head(dot(normed, key_matrix).astype(jnp.bfloat16))
    local_v = by_head(dot(normed, value_matrix).astype(jnp.bfloat16))
    spread = jnp.pad(
        normed.reshape(ROWS, DEVICES, QROWS), ((0, 0), (0, 0), (0, QPAD - QROWS))
    ).reshape(ROWS, DEVICES * QPAD)
    post = post_gain.reshape(1, WIDTH)
    gain = norm_gain.reshape(1, WIDTH)
    first = (lax.axis_index(SEG) == 0).astype(jnp.int32).reshape(1)
    q, newest, square = first_step(spread, local_k, local_v, memory, post, gathered)
    squares = [square]
    for step in range(1, ITERS):
        last = step + 1 == ITERS
        shifted = from_behind(newest, SEG, 1)
        outs = later_step(
            last, first, shifted, newest, memory, tokens, q, local_k, local_v, gain, post,
            key_matrix, value_matrix, gathered,
        )
        newest, square = outs[-2:]
        squares.append(square)
    own = jnp.stack([square[0, 0] for square in squares]) * segment_weight[0]
    row = jnp.pad(own, (0, 125)).reshape(1, 128)
    everyone = lax.all_to_all(
        jnp.broadcast_to(row, (DEVICES, 128)), SEG, split_axis=0, concat_axis=0, tiled=True
    )
    totals = jnp.sum(everyone, axis=0)[:ITERS]
    change_vec = jnp.sqrt(totals / (DEVICES * MEM * WIDTH) + eps)
    return (outs[0], newest, change_vec)


def solution(mesh):
    finer = Mesh(mesh.devices.reshape(4, 4, 4, 2), SEG)
    in_specs = (P(SEG, None), P(), P(), P(), P(SEG, None), P(), P(), P(SEG, None), P(SEG))
    out_specs = (P(SEG, None), P(SEG, None), P())
    return jax.shard_map(
        shards, mesh=finer, in_specs=in_specs, out_specs=out_specs, check_vma=False
    )
```

```python
import functools

import jax
import jax.numpy as jnp
from jax import lax
from jax.experimental import pallas as pl
from jax.experimental.pallas import tpu as pltpu
from jax.sharding import Mesh
from jax.sharding import PartitionSpec as P

HEAD = 256
GROUPS = 4
PAIR = 2 * HEAD
ITERS = 3
WIDTH = 3584
MEM = 64
TOK = 256
ROWS = TOK + MEM
CHUNKS = WIDTH // PAIR
QROWS = 28
QPAD = 32
OROWS = 16
DEVICES = 128
SEG = ("seg_0", "seg_1", "seg_2", "seg_3")
MIB = 1024 * 1024

eps = 1e-06


def from_behind(block, axis, distance):
    devices = range(lax.axis_size(axis))
    route = [(i - distance, i) for i in devices if i - distance in devices]
    return lax.ppermute(block, axis, route)


def prenorm(rows, gain):
    rows = rows.astype(jnp.float32)
    mean_sq = jnp.mean(rows * rows, axis=-1, keepdims=True)
    return (rows / jnp.sqrt(mean_sq + eps) * gain).astype(jnp.bfloat16)


def dot(a, b):
    return jnp.dot(a, b, preferred_element_type=jnp.float32)


def attend(q, keys, values, row0):
    rows = q.shape[0]
    both = jnp.concatenate([q[:, :HEAD], q[:, HEAD:]], axis=0)
    score = lax.dot_general(
        both, keys, (((1,), (1,)), ((), ())), preferred_element_type=jnp.float32
    )
    row = lax.broadcasted_iota(jnp.int32, score.shape, 0)
    row = jnp.where(row >= rows, row - rows, row) + row0
    col = lax.broadcasted_iota(jnp.int32, score.shape, 1)
    expo = jnp.where(col - MEM <= row, jnp.exp(score), 0.0)
    denom = jnp.sum(expo, axis=-1, keepdims=True)
    numer = dot(expo.astype(jnp.bfloat16), values)
    attn = (numer / denom).astype(jnp.bfloat16)
    return jnp.concatenate([attn[:rows], attn[rows:]], axis=1)


def project_out(attn_ref, weight_ref, proj_ref, ready=None):
    attn = jnp.concatenate([attn_ref[g] for g in range(GROUPS)], axis=1)
    total = jnp.zeros((attn.shape[0], 1), jnp.float32)
    for b in range(CHUNKS):
        if ready is not None:
            ready(b)
        proj = dot(attn, weight_ref[b].reshape(DEVICES * OROWS, PAIR))
        proj_ref[b] = proj
        total = total + jnp.sum(proj * proj, axis=-1, keepdims=True)
    return total


def finish_rows(proj_ref, start, count, total, residual_ref, gain_ref, out_ref):
    root = jnp.sqrt(total[start : start + count] * (1.0 / WIDTH) + eps)
    for b in range(CHUNKS):
        cols = slice(b * PAIR, (b + 1) * PAIR)
        proj = proj_ref[b, start : start + count, :]
        out = residual_ref[:, cols].astype(jnp.float32) + proj / root * gain_ref[:, cols]
        out_ref[:, cols] = out.astype(jnp.bfloat16)


def squared_change(new_ref, old_ref):
    total = jnp.zeros((MEM, PAIR), jnp.float32)
    for b in range(CHUNKS):
        cols = slice(b * PAIR, (b + 1) * PAIR)
        diff = new_ref[:, cols].astype(jnp.float32) - old_ref[:, cols].astype(jnp.float32)
        total = total + diff * diff
    return jnp.sum(total)


def pack_kernel(query_ref, output_ref, out_ref):
    for g in range(GROUPS):
        out_ref[g * QPAD : g * QPAD + QROWS, :] = query_ref[:, g * PAIR : (g + 1) * PAIR]
        out_ref[g * QPAD + QROWS : (g + 1) * QPAD, :] = jnp.zeros(
            (QPAD - QROWS, PAIR), jnp.bfloat16
        )
    for b in range(CHUNKS):
        first = GROUPS * QPAD + b * OROWS
        out_ref[first : first + OROWS, :] = output_ref[:, b * PAIR : (b + 1) * PAIR]


def first_kernel(
    normed_hbm, k_ref, v_ref, memory_ref, post_ref, first, gain, gathered,
    q_ref, new_ref, sq_ref, out_ref,
    wqbuf, normed_ref, attn_ref, proj_ref, wqsem, wosem, hsem,
):
    def q_copy(g):
        return pltpu.make_async_copy(
            gathered.at[:, pl.ds(g * QPAD, QPAD), :], wqbuf.at[g], wqsem.at[g]
        )

    def out_copy(b):
        return pltpu.make_async_copy(
            gathered.at[:, pl.ds(GROUPS * QPAD + b * OROWS, OROWS), :], out_ref.at[b], wosem.at[b]
        )

    rows_copy = pltpu.make_async_copy(normed_hbm, normed_ref, hsem)
    rows_copy.start()
    q_copy(0).start()
    q_copy(1).start()
    rows_copy.wait()
    for g in range(GROUPS):
        q_copy(g).wait()
        if g + 2 < GROUPS:
            q_copy(g + 2).start()
        for b in range(2 * g - 2, 2 * g):
            if b >= 0:
                out_copy(b).start()
        acc = dot(normed_ref[...], wqbuf[g].reshape(DEVICES * QPAD, PAIR))
        q = (acc * (1.0 / HEAD**0.5)).astype(jnp.bfloat16)
        q_ref[g] = q
        keys = k_ref[g]
        values = v_ref[g]
        keys = jnp.concatenate([keys[TOK:], keys], axis=0)
        values = jnp.concatenate([values[TOK:], values], axis=0)
        attn_ref[g] = attend(q[TOK:], keys, values, TOK)
    out_copy(CHUNKS - 1).start()
    total = project_out(attn_ref, out_ref, proj_ref, lambda b: out_copy(b).wait())
    finish_rows(proj_ref, 0, MEM, total, memory_ref, post_ref, new_ref)
    sq_ref[...] = jnp.full((8, 128), squared_change(new_ref, memory_ref), jnp.float32)


def step_kernel(
    last, first_ref, weight_ref, shifted_ref, previous_ref, memory_ref, tokens_ref, squares_ref,
    q_ref, k_ref, v_ref, gain_ref, post_ref, key_ref, value_ref, out_ref, *rest,
):
    if last:
        tok_ref = rest[0]
        rest = rest[1:]
    new_ref, sq_ref, normed_ref, attn_ref, proj_ref = rest
    at_start = first_ref[0] == 1

    def read_rows(i):
        cols = slice(i * PAIR, (i + 1) * PAIR)
        return jnp.where(at_start, memory_ref[:, cols], shifted_ref[:, cols]).astype(jnp.float32)

    total = jnp.zeros((MEM, 1), jnp.float32)
    for i in range(CHUNKS):
        rows = read_rows(i)
        total = total + jnp.sum(rows * rows, axis=-1, keepdims=True)
    root = jnp.sqrt(total * (1.0 / WIDTH) + eps)
    for i in range(CHUNKS):
        cols = slice(i * PAIR, (i + 1) * PAIR)
        normed_ref[:, cols] = (read_rows(i) / root * gain_ref[:, cols]).astype(jnp.bfloat16)
    row0 = 0 if last else TOK
    normed = normed_ref[...]
    for g in range(GROUPS):
        cols = slice(g * HEAD, (g + 1) * HEAD)
        read_k = dot(normed, key_ref[:, cols]).astype(jnp.bfloat16)
        read_v = dot(normed, value_ref[:, cols]).astype(jnp.bfloat16)
        keys = jnp.concatenate([read_k, k_ref[g]], axis=0)
        values = jnp.concatenate([read_v, v_ref[g]], axis=0)
        attn_ref[g] = attend(q_ref[g, row0:, :], keys, values, row0)
    total = project_out(attn_ref, out_ref, proj_ref)
    start = 0
    if last:
        finish_rows(proj_ref, 0, TOK, total, tokens_ref, post_ref, tok_ref)
        start = TOK
    finish_rows(proj_ref, start, MEM, total, memory_ref, post_ref, new_ref)
    change = squared_change(new_ref, previous_ref)
    earlier = squares_ref[...]
    if last:
        lane = lax.broadcasted_iota(jnp.int32, (8, 128), 1)
        row = jnp.where(lane == 2, change, earlier) * weight_ref[0]
        for i in range(DEVICES // 8):
            sq_ref[8 * i : 8 * (i + 1), :] = row
    else:
        lane = lax.broadcasted_iota(jnp.int32, (8, 128), 1)
        sq_ref[...] = jnp.where(lane == 0, earlier, change)


def whole():
    return pl.BlockSpec(memory_space=pltpu.VMEM)


def in_hbm():
    return pl.BlockSpec(memory_space=pltpu.HBM)


def in_smem():
    return pl.BlockSpec(memory_space=pltpu.SMEM)


def params(mib):
    return pltpu.CompilerParams(vmem_limit_bytes=mib * MIB)


def far(x):
    return pltpu.with_memory_space_constraint(x, pltpu.HBM)


def pinned(x):
    return pltpu.with_memory_space_constraint(x, pltpu.VMEM)


def pack(query_weight, output_weight):
    return pl.pallas_call(
        pack_kernel,
        name="pack",
        out_shape=jax.ShapeDtypeStruct((GROUPS * QPAD + CHUNKS * OROWS, PAIR), jnp.bfloat16),
        in_specs=[whole(), whole()],
        out_specs=whole(),
        compiler_params=params(2),
    )(query_weight, output_weight)


def first_step(normed, k, v, memory, post_gain, first, gain, gathered):
    return pl.pallas_call(
        first_kernel,
        name="first_step",
        out_shape=(
            jax.ShapeDtypeStruct((GROUPS, ROWS, PAIR), jnp.bfloat16),
            jax.ShapeDtypeStruct((MEM, WIDTH), jnp.bfloat16),
            jax.ShapeDtypeStruct((8, 128), jnp.float32),
            pltpu.VMEM((CHUNKS, DEVICES, OROWS, PAIR), jnp.bfloat16),
        ),
        in_specs=[in_hbm()]
        + [whole()] * 4
        + [in_smem(), pl.BlockSpec(memory_space=pl.ANY), in_hbm()],
        out_specs=(whole(), whole(), whole(), whole()),
        scratch_shapes=[
            pltpu.VMEM((GROUPS, DEVICES, QPAD, PAIR), jnp.bfloat16),
            pltpu.VMEM((ROWS, DEVICES * QPAD), jnp.bfloat16),
            pltpu.VMEM((GROUPS, MEM, PAIR), jnp.bfloat16),
            pltpu.VMEM((CHUNKS, MEM, PAIR), jnp.float32),
            pltpu.SemaphoreType.DMA((GROUPS,)),
            pltpu.SemaphoreType.DMA((CHUNKS,)),
            pltpu.SemaphoreType.DMA,
        ],
        compiler_params=params(24),
    )(normed, k, v, memory, post_gain, first, gain, gathered)


def later_step(
    last, first, weight, shifted, previous, memory, tokens, squares, q, k, v, gain, post_gain,
    key_matrix, value_matrix, out_matrix,
):
    rows = ROWS if last else MEM
    out_shape = [
        jax.ShapeDtypeStruct((MEM, WIDTH), jnp.bfloat16),
        jax.ShapeDtypeStruct((DEVICES if last else 8, 128), jnp.float32),
    ]
    if last:
        out_shape = [jax.ShapeDtypeStruct((TOK, WIDTH), jnp.bfloat16)] + out_shape
    return pl.pallas_call(
        functools.partial(step_kernel, last),
        name="last_step" if last else "middle_step",
        out_shape=tuple(out_shape),
        in_specs=[in_smem(), in_smem()]
        + [whole()] * 3
        + [whole() if last else in_hbm()]
        + [whole()] * 9,
        out_specs=tuple(whole() for _ in out_shape),
        scratch_shapes=[
            pltpu.VMEM((MEM, WIDTH), jnp.bfloat16),
            pltpu.VMEM((GROUPS, rows, PAIR), jnp.bfloat16),
            pltpu.VMEM((CHUNKS, rows, PAIR), jnp.float32),
        ],
        compiler_params=params(16 if last else 8),
    )(first, weight, shifted, previous, memory, tokens, squares, q, k, v, gain, post_gain,
      key_matrix, value_matrix, pinned(out_matrix))


def by_head(x):
    return jnp.transpose(x.reshape(x.shape[0], GROUPS, HEAD), (1, 0, 2))


def shards(
    tokens,
    memory,
    norm_gain,
    post_gain,
    query_weight,
    key_matrix,
    value_matrix,
    output_weight,
    segment_weight,
):
    mine = pack(query_weight, output_weight)
    gathered = lax.all_gather(mine, SEG, axis=0, tiled=False)
    inputs = jnp.concatenate([tokens, memory], axis=0)
    normed = prenorm(inputs, norm_gain)
    local_k = by_head(dot(normed, key_matrix).astype(jnp.bfloat16))
    local_v = by_head(dot(normed, value_matrix).astype(jnp.bfloat16))
    spread = jnp.pad(
        normed.reshape(ROWS, DEVICES, QROWS), ((0, 0), (0, 0), (0, QPAD - QROWS))
    ).reshape(ROWS, DEVICES * QPAD)
    post = post_gain.reshape(1, WIDTH)
    gain = norm_gain.reshape(1, WIDTH)
    first = (lax.axis_index(SEG) == 0).astype(jnp.int32).reshape(1)
    keys_near, values_near = pinned(key_matrix), pinned(value_matrix)
    q, newest, squares, out_near = first_step(far(spread), local_k, local_v, memory, post, first, gain, gathered)
    for step in range(1, ITERS):
        last = step + 1 == ITERS
        shifted = from_behind(newest, SEG, 1)
        outs = later_step(
            last, first, segment_weight, shifted, newest, memory, tokens, squares, q,
            local_k, local_v, gain, post, keys_near, values_near, out_near,
        )
        newest, squares = outs[-2:]
    everyone = lax.all_to_all(
        squares, SEG, split_axis=0, concat_axis=0, tiled=True
    )
    totals = jnp.sum(everyone, axis=0)[:ITERS]
    change_vec = jnp.sqrt(totals / (DEVICES * MEM * WIDTH) + eps)
    return (outs[0], newest, change_vec)


def solution(mesh):
    finer = Mesh(mesh.devices.reshape(4, 4, 4, 2), SEG)
    in_specs = (P(SEG, None), P(), P(), P(), P(SEG, None), P(), P(), P(SEG, None), P(SEG))
    out_specs = (P(SEG, None), P(SEG, None), P())
    return jax.shard_map(
        shards, mesh=finer, in_specs=in_specs, out_specs=out_specs, check_vma=False
    )
```

```python
import functools

import jax
import jax.numpy as jnp
from jax import lax
from jax.experimental import pallas as pl
from jax.experimental.pallas import tpu as pltpu
from jax.sharding import Mesh
from jax.sharding import PartitionSpec as P

HEAD = 256
GROUPS = 4
PAIR = 2 * HEAD
ITERS = 3
WIDTH = 3584
MEM = 64
TOK = 256
ROWS = TOK + MEM
CHUNKS = WIDTH // PAIR
QROWS = 28
MAIN = 24
REST = QROWS - MAIN
OROWS = 16
DEVICES = 128
QBLOCK = 2 * QROWS
OFIRST = GROUPS * QROWS
PACKED = OFIRST + CHUNKS * OROWS
SEG = ("seg_0", "seg_1", "seg_2", "seg_3")
MIB = 1024 * 1024

eps = 1e-06


def from_behind(block, axis, distance):
    devices = range(lax.axis_size(axis))
    route = [(i - distance, i) for i in devices if i - distance in devices]
    return lax.ppermute(block, axis, route)


def prenorm(rows, gain):
    rows = rows.astype(jnp.float32)
    mean_sq = jnp.mean(rows * rows, axis=-1, keepdims=True)
    return (rows / jnp.sqrt(mean_sq + eps) * gain).astype(jnp.bfloat16)


def dot(a, b):
    return jnp.dot(a, b, preferred_element_type=jnp.float32)


def attend(q, keys, values, row0):
    rows = q.shape[0]
    both = jnp.concatenate([q[:, :HEAD], q[:, HEAD:]], axis=0)
    score = lax.dot_general(
        both, keys, (((1,), (1,)), ((), ())), preferred_element_type=jnp.float32
    )
    row = lax.broadcasted_iota(jnp.int32, score.shape, 0)
    row = jnp.where(row >= rows, row - rows, row) + row0
    col = lax.broadcasted_iota(jnp.int32, score.shape, 1)
    expo = jnp.where(col - MEM <= row, jnp.exp(score), 0.0)
    denom = jnp.sum(expo, axis=-1, keepdims=True)
    numer = dot(expo.astype(jnp.bfloat16), values)
    attn = (numer / denom).astype(jnp.bfloat16)
    return jnp.concatenate([attn[:rows], attn[rows:]], axis=1)


def project_out(attn_ref, weight_ref, proj_ref, ready=None):
    attn = jnp.concatenate([attn_ref[g] for g in range(GROUPS)], axis=1)
    total = jnp.zeros((attn.shape[0], 1), jnp.float32)
    for b in range(CHUNKS):
        if ready is not None:
            ready(b)
        proj = dot(attn, weight_ref[b].reshape(DEVICES * OROWS, PAIR))
        proj_ref[b] = proj
        total = total + jnp.sum(proj * proj, axis=-1, keepdims=True)
    return total


def finish_rows(proj_ref, start, count, total, residual_ref, gain_ref, out_ref):
    root = jnp.sqrt(total[start : start + count] * (1.0 / WIDTH) + eps)
    for b in range(CHUNKS):
        cols = slice(b * PAIR, (b + 1) * PAIR)
        proj = proj_ref[b, start : start + count, :]
        out = residual_ref[:, cols].astype(jnp.float32) + proj / root * gain_ref[:, cols]
        out_ref[:, cols] = out.astype(jnp.bfloat16)


def squared_change(new_ref, old_ref):
    total = jnp.zeros((MEM, PAIR), jnp.float32)
    for b in range(CHUNKS):
        cols = slice(b * PAIR, (b + 1) * PAIR)
        diff = new_ref[:, cols].astype(jnp.float32) - old_ref[:, cols].astype(jnp.float32)
        total = total + diff * diff
    return jnp.sum(total)


def pack_kernel(query_hbm, output_hbm, out_ref, query_ref, output_ref, qsem, osem):
    query_copy = pltpu.make_async_copy(query_hbm, query_ref, qsem)
    output_copy = pltpu.make_async_copy(output_hbm, output_ref, osem)
    query_copy.start()
    output_copy.start()
    query_copy.wait()
    for g in range(GROUPS):
        cols = slice(g * PAIR, (g + 1) * PAIR)
        base = (g // 2) * QBLOCK
        main = base + (g % 2) * MAIN
        rest = base + 2 * MAIN + (g % 2) * REST
        out_ref[main : main + MAIN, :] = query_ref[:MAIN, cols]
        out_ref[rest : rest + REST, :] = query_ref[MAIN:, cols]
    output_copy.wait()
    for b in range(CHUNKS):
        first = OFIRST + b * OROWS
        out_ref[first : first + OROWS, :] = output_ref[:, b * PAIR : (b + 1) * PAIR]


def project_read(new_ref, gain_ref, normed_ref, key_ref, value_ref, kv_ref, ready=None):
    total = jnp.zeros((MEM, 1), jnp.float32)
    for i in range(CHUNKS):
        rows = new_ref[:, i * PAIR : (i + 1) * PAIR].astype(jnp.float32)
        total = total + jnp.sum(rows * rows, axis=-1, keepdims=True)
    root = jnp.sqrt(total * (1.0 / WIDTH) + eps)
    for i in range(CHUNKS):
        cols = slice(i * PAIR, (i + 1) * PAIR)
        rows = new_ref[:, cols].astype(jnp.float32)
        normed_ref[:, cols] = (rows / root * gain_ref[:, cols]).astype(jnp.bfloat16)
    normed = normed_ref[...]
    for part, weight_ref in enumerate((key_ref, value_ref)):
        if ready is not None:
            ready(part)
        for g in range(GROUPS):
            cols = slice(g * HEAD, (g + 1) * HEAD)
            kv_ref[g, :, part * HEAD : (part + 1) * HEAD] = dot(normed, weight_ref[:, cols]).astype(
                jnp.bfloat16
            )


def first_kernel(
    main_hbm, even_hbm, odd_hbm, memory_hbm, k_ref, v_ref, gain_ref, post_ref, first,
    key_hbm, value_hbm, gathered,
    q_ref, new_ref, kv_ref, sq_ref, key_ref, value_ref, out_ref,
    main_ref, even_ref, odd_ref, memory_ref, wmain, wrest, attn_ref, proj_ref, normed_ref,
    rowsem, mainsem, restsem, outsem, kvsem,
):
    def rows_copy(i):
        source = (main_hbm, even_hbm, odd_hbm, memory_hbm)[i]
        return pltpu.make_async_copy(
            source, (main_ref, even_ref, odd_ref, memory_ref)[i], rowsem.at[i]
        )

    def main_copy(g):
        start = (g // 2) * QBLOCK + (g % 2) * MAIN
        return pltpu.make_async_copy(
            gathered.at[:, pl.ds(start, MAIN), :], wmain.at[g], mainsem.at[g]
        )

    def rest_copy(i):
        start = i * QBLOCK + 2 * MAIN
        return pltpu.make_async_copy(
            gathered.at[:, pl.ds(start, 2 * REST), :], wrest.at[i], restsem.at[i]
        )

    def out_copy(b):
        return pltpu.make_async_copy(
            gathered.at[:, pl.ds(OFIRST + b * OROWS, OROWS), :], out_ref.at[b], outsem.at[b]
        )

    def kv_copy(i):
        source, target = ((key_hbm, key_ref), (value_hbm, value_ref))[i]
        return pltpu.make_async_copy(source, target, kvsem.at[i])

    waiting = [rest_copy(0), main_copy(0), main_copy(1), rest_copy(1), main_copy(2), main_copy(3)]
    waiting += [out_copy(b) for b in range(CHUNKS)] + [kv_copy(0), kv_copy(1)]
    waiting.reverse()

    def start(count):
        for _ in range(count):
            if waiting:
                waiting.pop().start()

    for i in range(4):
        rows_copy(i).start()
    start(3)
    for i in range(4):
        rows_copy(i).wait()
    for g in range(GROUPS):
        if g % 2 == 0:
            rest_copy(g // 2).wait()
        main_copy(g).wait()
        start(2)
        acc = dot(main_ref[...], wmain[g].reshape(DEVICES * MAIN, PAIR))
        rest_rows = (even_ref if g % 2 == 0 else odd_ref)[...]
        acc = acc + dot(rest_rows, wrest[g // 2].reshape(DEVICES * 2 * REST, PAIR))
        q = (acc * (1.0 / HEAD**0.5)).astype(jnp.bfloat16)
        q_ref[g] = q
        keys = k_ref[g]
        values = v_ref[g]
        keys = jnp.concatenate([keys[TOK:], keys], axis=0)
        values = jnp.concatenate([values[TOK:], values], axis=0)
        attn_ref[g] = attend(q[TOK:], keys, values, TOK)

    def out_ready(b):
        out_copy(b).wait()
        start(1)

    total = project_out(attn_ref, out_ref, proj_ref, out_ready)
    start(len(waiting))
    finish_rows(proj_ref, 0, MEM, total, memory_ref, post_ref, new_ref)
    project_read(
        new_ref, gain_ref, normed_ref, key_ref, value_ref, kv_ref, lambda i: kv_copy(i).wait()
    )
    sq_ref[...] = jnp.full((8, 128), squared_change(new_ref, memory_ref), jnp.float32)


def step_kernel(
    last, first_ref, weight_ref, shifted_ref, previous_ref, memory_ref, tokens_ref, squares_ref,
    q_ref, k_ref, v_ref, gain_ref, post_ref, *rest,
):
    if last:
        out_ref, tok_ref, new_ref, sq_ref, attn_ref, proj_ref = rest
    else:
        key_ref, value_ref, out_ref, new_ref, kv_ref, sq_ref, attn_ref, proj_ref, normed_ref = rest
    at_start = first_ref[0] == 1
    row0 = 0 if last else TOK
    for g in range(GROUPS):
        read_k = jnp.where(at_start, k_ref[g, TOK:, :], shifted_ref[g, :, :HEAD])
        read_v = jnp.where(at_start, v_ref[g, TOK:, :], shifted_ref[g, :, HEAD:])
        keys = jnp.concatenate([read_k, k_ref[g]], axis=0)
        values = jnp.concatenate([read_v, v_ref[g]], axis=0)
        attn_ref[g] = attend(q_ref[g, row0:, :], keys, values, row0)
    total = project_out(attn_ref, out_ref, proj_ref)
    start = 0
    if last:
        finish_rows(proj_ref, 0, TOK, total, tokens_ref, post_ref, tok_ref)
        start = TOK
    finish_rows(proj_ref, start, MEM, total, memory_ref, post_ref, new_ref)
    if not last:
        project_read(new_ref, gain_ref, normed_ref, key_ref, value_ref, kv_ref)
    change = squared_change(new_ref, previous_ref)
    earlier = squares_ref[...]
    lane = lax.broadcasted_iota(jnp.int32, (8, 128), 1)
    if last:
        row = jnp.where(lane == 2, change, earlier) * weight_ref[0]
        for i in range(DEVICES // 8):
            sq_ref[8 * i : 8 * (i + 1), :] = row
    else:
        sq_ref[...] = jnp.where(lane == 0, earlier, change)


def whole():
    return pl.BlockSpec(memory_space=pltpu.VMEM)


def in_hbm():
    return pl.BlockSpec(memory_space=pltpu.HBM)


def in_smem():
    return pl.BlockSpec(memory_space=pltpu.SMEM)


def params(mib):
    return pltpu.CompilerParams(vmem_limit_bytes=mib * MIB)


def far(x):
    return pltpu.with_memory_space_constraint(x, pltpu.HBM)


def pinned(x):
    return pltpu.with_memory_space_constraint(x, pltpu.VMEM)


def pack(query_weight, output_weight):
    return pl.pallas_call(
        pack_kernel,
        name="pack",
        out_shape=jax.ShapeDtypeStruct((PACKED, PAIR), jnp.bfloat16),
        in_specs=[in_hbm(), in_hbm()],
        out_specs=whole(),
        scratch_shapes=[
            pltpu.VMEM((QROWS, GROUPS * PAIR), jnp.bfloat16),
            pltpu.VMEM((OROWS, WIDTH), jnp.bfloat16),
            pltpu.SemaphoreType.DMA,
            pltpu.SemaphoreType.DMA,
        ],
        compiler_params=params(2),
    )(far(query_weight), far(output_weight))


READ = jax.ShapeDtypeStruct((GROUPS, MEM, PAIR), jnp.bfloat16)
WRITTEN = jax.ShapeDtypeStruct((MEM, WIDTH), jnp.bfloat16)


def first_step(main, even, odd, memory, k, v, gain, post_gain, first, key_matrix, value_matrix,
               gathered):
    near = pltpu.VMEM((WIDTH, GROUPS * HEAD), jnp.bfloat16)
    return pl.pallas_call(
        first_kernel,
        name="first_step",
        out_shape=(
            jax.ShapeDtypeStruct((GROUPS, ROWS, PAIR), jnp.bfloat16),
            WRITTEN,
            READ,
            jax.ShapeDtypeStruct((8, 128), jnp.float32),
            near,
            near,
            pltpu.VMEM((CHUNKS, DEVICES, OROWS, PAIR), jnp.bfloat16),
        ),
        in_specs=[in_hbm()] * 4 + [whole()] * 4 + [in_smem()] + [in_hbm()] * 3,
        out_specs=tuple(whole() for _ in range(7)),
        scratch_shapes=[
            pltpu.VMEM((ROWS, DEVICES * MAIN), jnp.bfloat16),
            pltpu.VMEM((ROWS, DEVICES * 2 * REST), jnp.bfloat16),
            pltpu.VMEM((ROWS, DEVICES * 2 * REST), jnp.bfloat16),
            pltpu.VMEM((MEM, WIDTH), jnp.bfloat16),
            pltpu.VMEM((GROUPS, DEVICES, MAIN, PAIR), jnp.bfloat16),
            pltpu.VMEM((2, DEVICES, 2 * REST, PAIR), jnp.bfloat16),
            pltpu.VMEM((GROUPS, MEM, PAIR), jnp.bfloat16),
            pltpu.VMEM((CHUNKS, MEM, PAIR), jnp.float32),
            pltpu.VMEM((MEM, WIDTH), jnp.bfloat16),
            pltpu.SemaphoreType.DMA((4,)),
            pltpu.SemaphoreType.DMA((GROUPS,)),
            pltpu.SemaphoreType.DMA((2,)),
            pltpu.SemaphoreType.DMA((CHUNKS,)),
            pltpu.SemaphoreType.DMA((2,)),
        ],
        compiler_params=params(20),
    )(far(main), far(even), far(odd), far(memory), k, v, gain, post_gain, first,
      far(key_matrix), far(value_matrix), gathered)


def later_step(last, first, weight, shifted, previous, memory, tokens, squares, q, k, v, gain,
               post_gain, *weights):
    rows = ROWS if last else MEM
    if last:
        out_shape = (
            jax.ShapeDtypeStruct((TOK, WIDTH), jnp.bfloat16),
            WRITTEN,
            jax.ShapeDtypeStruct((DEVICES, 128), jnp.float32),
        )
    else:
        out_shape = (WRITTEN, READ, jax.ShapeDtypeStruct((8, 128), jnp.float32))
    scratch = [
        pltpu.VMEM((GROUPS, rows, PAIR), jnp.bfloat16),
        pltpu.VMEM((CHUNKS, rows, PAIR), jnp.float32),
    ]
    if not last:
        scratch.append(pltpu.VMEM((MEM, WIDTH), jnp.bfloat16))
    return pl.pallas_call(
        functools.partial(step_kernel, last),
        name="last_step" if last else "middle_step",
        out_shape=out_shape,
        in_specs=[in_smem(), in_smem()]
        + [whole()] * 3
        + [whole() if last else pl.BlockSpec(memory_space=pl.ANY)]
        + [whole()] * (6 + len(weights)),
        out_specs=(whole(), whole(), whole()),
        scratch_shapes=scratch,
        compiler_params=params(10 if last else 3),
    )(first, weight, shifted, previous, memory, tokens, squares, q, k, v, gain, post_gain,
      *(pinned(x) for x in weights))


def by_head(x):
    return jnp.transpose(x.reshape(x.shape[0], GROUPS, HEAD), (1, 0, 2))


def shards(
    tokens,
    memory,
    norm_gain,
    post_gain,
    query_weight,
    key_matrix,
    value_matrix,
    output_weight,
    segment_weight,
):
    mine = pack(query_weight, output_weight)
    gathered = lax.all_gather(mine, SEG, axis=0, tiled=False)
    inputs = jnp.concatenate([tokens, memory], axis=0)
    normed = prenorm(inputs, norm_gain)
    local_k = by_head(dot(normed, key_matrix).astype(jnp.bfloat16))
    local_v = by_head(dot(normed, value_matrix).astype(jnp.bfloat16))
    by_device = normed.reshape(ROWS, DEVICES, QROWS)
    main = by_device[:, :, :MAIN].reshape(ROWS, DEVICES * MAIN)
    rest = by_device[:, :, MAIN:]
    even = jnp.pad(rest, ((0, 0), (0, 0), (0, REST))).reshape(ROWS, DEVICES * 2 * REST)
    odd = jnp.pad(rest, ((0, 0), (0, 0), (REST, 0))).reshape(ROWS, DEVICES * 2 * REST)
    post = post_gain.reshape(1, WIDTH)
    gain = norm_gain.reshape(1, WIDTH)
    first = (lax.axis_index(SEG) == 0).astype(jnp.int32).reshape(1)
    q, newest, read, squares, near_k, near_v, near_out = first_step(
        main, even, odd, memory, local_k, local_v, gain, post, first, key_matrix, value_matrix,
        gathered,
    )

    def later(last, shifted, weights):
        return later_step(
            last, first, segment_weight, shifted, newest, memory, tokens, squares, q,
            local_k, local_v, gain, post, *weights,
        )

    shifted = from_behind(read, SEG, 1)
    newest, read, squares = later(False, shifted, (near_k, near_v, near_out))
    shifted = from_behind(read, SEG, 1)
    token_out, newest, squares = later(True, shifted, (near_out,))
    everyone = lax.all_to_all(
        squares, SEG, split_axis=0, concat_axis=0, tiled=True
    )
    totals = jnp.sum(everyone, axis=0)[:ITERS]
    change_vec = jnp.sqrt(totals / (DEVICES * MEM * WIDTH) + eps)
    return (token_out, newest, change_vec)


def solution(mesh):
    finer = Mesh(mesh.devices.reshape(4, 4, 4, 2), SEG)
    in_specs = (P(SEG, None), P(), P(), P(), P(SEG, None), P(), P(), P(SEG, None), P(SEG))
    out_specs = (P(SEG, None), P(SEG, None), P())
    return jax.shard_map(
        shards, mesh=finer, in_specs=in_specs, out_specs=out_specs, check_vma=False
    )
```

```python
import functools

import jax
import jax.numpy as jnp
from jax import lax
from jax.experimental import pallas as pl
from jax.experimental.pallas import tpu as pltpu
from jax.sharding import Mesh
from jax.sharding import PartitionSpec as P

HEAD = 256
GROUPS = 4
PAIR = 2 * HEAD
ITERS = 3
WIDTH = 3584
MEM = 64
TOK = 256
ROWS = TOK + MEM
CHUNKS = WIDTH // PAIR
QROWS = 28
MAIN = 24
REST = QROWS - MAIN
OROWS = 16
DEVICES = 128
QBLOCK = 2 * QROWS
OFIRST = GROUPS * QROWS
PACKED = OFIRST + CHUNKS * OROWS
SEG = ("seg_0", "seg_1", "seg_2", "seg_3")
MIB = 1024 * 1024

eps = 1e-06


def from_behind(block, axis, distance):
    devices = range(lax.axis_size(axis))
    route = [(i - distance, i) for i in devices if i - distance in devices]
    return lax.ppermute(block, axis, route)


def prenorm(rows, gain):
    rows = rows.astype(jnp.float32)
    mean_sq = jnp.mean(rows * rows, axis=-1, keepdims=True)
    return (rows / jnp.sqrt(mean_sq + eps) * gain).astype(jnp.bfloat16)


def dot(a, b):
    return jnp.dot(a, b, preferred_element_type=jnp.float32)


def attend(q, read, tokens, memory, row0):
    rows = q.shape[0]
    kv = jnp.concatenate([read, tokens, memory], axis=0)
    keys = kv[:, :HEAD]
    values = kv[:, HEAD:]
    both = jnp.concatenate([q[:, :HEAD], q[:, HEAD:]], axis=0)
    score = lax.dot_general(
        both, keys, (((1,), (1,)), ((), ())), preferred_element_type=jnp.float32
    )
    row = lax.broadcasted_iota(jnp.int32, score.shape, 0)
    row = jnp.where(row >= rows, row - rows, row) + row0
    col = lax.broadcasted_iota(jnp.int32, score.shape, 1)
    expo = jnp.where(col - MEM <= row, jnp.exp(score), 0.0)
    denom = jnp.sum(expo, axis=-1, keepdims=True)
    numer = dot(expo.astype(jnp.bfloat16), values)
    attn = (numer / denom).astype(jnp.bfloat16)
    return jnp.concatenate([attn[:rows], attn[rows:]], axis=1)


def row_blocks(attn_ref):
    return jnp.concatenate([attn_ref[g] for g in range(GROUPS)], axis=1)


def project_out(attn, weight_ref, proj_ref, ready=None):
    total = jnp.zeros((attn.shape[0], 1), jnp.float32)
    for b in range(CHUNKS):
        if ready is not None:
            ready(b)
        proj = dot(attn, weight_ref[b].reshape(DEVICES * OROWS, PAIR))
        proj_ref[b] = proj
        total = total + jnp.sum(proj * proj, axis=-1, keepdims=True)
    return total


def finish_rows(proj_ref, start, count, total, residual_ref, gain_ref, out_ref, at=0):
    root = jnp.sqrt(total[start : start + count] * (1.0 / WIDTH) + eps)
    for b in range(CHUNKS):
        cols = slice(b * PAIR, (b + 1) * PAIR)
        proj = proj_ref[b, start : start + count, :]
        out = residual_ref[:, cols].astype(jnp.float32) + proj / root * gain_ref[:, cols]
        out_ref[at : at + count, cols] = out.astype(jnp.bfloat16)


def squared_change(new_ref, old_ref):
    total = jnp.zeros((MEM, PAIR), jnp.float32)
    for b in range(CHUNKS):
        cols = slice(b * PAIR, (b + 1) * PAIR)
        diff = new_ref[:, cols].astype(jnp.float32) - old_ref[:, cols].astype(jnp.float32)
        total = total + diff * diff
    return jnp.sum(total)


def pack_kernel(query_hbm, output_hbm, out_ref, query_ref, output_ref, qsem, osem):
    query_copy = pltpu.make_async_copy(query_hbm, query_ref, qsem)
    output_copy = pltpu.make_async_copy(output_hbm, output_ref, osem)
    query_copy.start()
    output_copy.start()
    query_copy.wait()
    for g in range(GROUPS):
        cols = slice(g * PAIR, (g + 1) * PAIR)
        base = (g // 2) * QBLOCK
        main = base + (g % 2) * MAIN
        rest = base + 2 * MAIN + (g % 2) * REST
        out_ref[main : main + MAIN, :] = query_ref[:MAIN, cols]
        out_ref[rest : rest + REST, :] = query_ref[MAIN:, cols]
    output_copy.wait()
    for b in range(CHUNKS):
        first = OFIRST + b * OROWS
        out_ref[first : first + OROWS, :] = output_ref[:, b * PAIR : (b + 1) * PAIR]


def project_read(new_ref, gain_ref, key_ref, value_ref, kv_ref, ready=None):
    total = jnp.zeros((new_ref.shape[0], 1), jnp.float32)
    for i in range(CHUNKS):
        rows = new_ref[:, i * PAIR : (i + 1) * PAIR].astype(jnp.float32)
        total = total + jnp.sum(rows * rows, axis=-1, keepdims=True)
    root = jnp.sqrt(total * (1.0 / WIDTH) + eps)
    for i in range(CHUNKS):
        cols = slice(i * PAIR, (i + 1) * PAIR)
        rows = new_ref[:, cols].astype(jnp.float32)
        new_ref[:, cols] = (rows / root * gain_ref[:, cols]).astype(jnp.bfloat16)
    normed = new_ref[...]
    for g in range(GROUPS):
        cols = slice(g * HEAD, (g + 1) * HEAD)
        if ready is not None:
            ready(g)
        kv_ref[g, :, :HEAD] = dot(normed, key_ref[:, cols]).astype(jnp.bfloat16)
        kv_ref[g, :, HEAD:] = dot(normed, value_ref[:, cols]).astype(jnp.bfloat16)


SLOTS = 2


def first_kernel(
    main_hbm, even_hbm, odd_hbm, memory_hbm, kv_hbm, behind1_hbm, behind2_hbm, gain_ref, post_ref,
    segment, key_hbm, value_hbm, gathered,
    q_ref, new_ref, read_ref, sq_ref, key_ref, value_ref, out_ref,
    main_ref, even_ref, odd_ref, memory_ref, memory_kv_ref, tokens_kv_ref,
    wmain, wrest, attn_ref, proj_ref, others_ref,
    rowsem, mainsem, restsem, outsem, kvsem,
):
    def rows_copy(i):
        source, target = (
            (main_hbm, main_ref),
            (even_hbm, even_ref),
            (odd_hbm, odd_ref),
            (kv_hbm.at[:, pl.ds(0, TOK), :], tokens_kv_ref.at[0]),
            (behind1_hbm, tokens_kv_ref.at[1]),
            (behind2_hbm, tokens_kv_ref.at[2]),
            (kv_hbm.at[:, pl.ds(TOK, MEM), :], memory_kv_ref),
            (memory_hbm, memory_ref),
        )[i]
        return pltpu.make_async_copy(source, target, rowsem.at[i])

    def main_copy(g):
        start = (g // 2) * QBLOCK + (g % 2) * MAIN
        return pltpu.make_async_copy(
            gathered.at[:, pl.ds(start, MAIN), :], wmain.at[g % SLOTS], mainsem.at[g]
        )

    def rest_copy(i):
        start = i * QBLOCK + 2 * MAIN
        return pltpu.make_async_copy(
            gathered.at[:, pl.ds(start, 2 * REST), :], wrest.at[i], restsem.at[i]
        )

    def out_copy(b):
        return pltpu.make_async_copy(
            gathered.at[:, pl.ds(OFIRST + b * OROWS, OROWS), :], out_ref.at[b], outsem.at[b]
        )

    def kv_copy(i):
        source, target = ((key_hbm, key_ref), (value_hbm, value_ref))[i % 2]
        cols = pl.ds((i // 2) * HEAD, HEAD)
        return pltpu.make_async_copy(source.at[:, cols], target.at[:, cols], kvsem.at[i])

    waiting = [rest_copy(0), main_copy(0)] + [rows_copy(i) for i in range(3, 8)]
    waiting += [main_copy(1), rest_copy(1), out_copy(0)]
    waiting += [main_copy(2), out_copy(1), out_copy(2), main_copy(3)]
    waiting += [out_copy(b) for b in range(3, CHUNKS)] + [kv_copy(i) for i in range(2 * GROUPS)]
    waiting.reverse()

    def start(count):
        for _ in range(min(count, len(waiting))):
            waiting.pop().start()

    for i in range(3):
        rows_copy(i).start()
    start(10)
    for i in range(3):
        rows_copy(i).wait()
    for g in range(GROUPS):
        if g % 2 == 0:
            rest_copy(g // 2).wait()
        main_copy(g).wait()
        acc = dot(main_ref[...], wmain[g % SLOTS].reshape(DEVICES * MAIN, PAIR))
        rest_rows = (even_ref if g % 2 == 0 else odd_ref)[...]
        acc = acc + dot(rest_rows, wrest[g // 2].reshape(DEVICES * 2 * REST, PAIR))
        q = (acc * (1.0 / HEAD**0.5)).astype(jnp.bfloat16)
        q_ref[g] = q
        if g == 0:
            for i in range(3, 7):
                rows_copy(i).wait()
        start(3)
        memory_kv = memory_kv_ref[g]

        def segments(i, _):
            attn_ref[i, g] = attend(q[TOK:], memory_kv, tokens_kv_ref[i, g], memory_kv, TOK)
            return 0

        lax.fori_loop(0, 3, segments, 0)

    def out_ready(b):
        out_copy(b).wait()
        start(1)

    attn = jnp.concatenate([row_blocks(attn_ref.at[i]) for i in range(3)], axis=0)
    total = project_out(attn, out_ref, proj_ref, out_ready)
    start(len(waiting))
    rows_copy(7).wait()
    for i in range(1, 3):
        finish_rows(
            proj_ref, i * MEM, MEM, total, memory_ref, post_ref, others_ref, (i - 1) * MEM
        )

    def kv_ready(g):
        kv_copy(2 * g).wait()
        kv_copy(2 * g + 1).wait()

    finish_rows(proj_ref, 0, MEM, total, memory_ref, post_ref, new_ref)
    sq_ref[...] = jnp.full((8, 128), squared_change(new_ref, memory_ref), jnp.float32)
    project_read(others_ref, gain_ref, key_ref, value_ref, read_ref, kv_ready)


def middle_kernel(
    segment, previous_ref, memory_ref, squares_ref, q_ref, kv_ref, behind1_ref, read_ref,
    gain_ref, post_ref, key_ref, value_ref, out_ref,
    new_ref, next_ref, sq_ref,
    attn_ref, proj_ref, other_ref,
):
    for g in range(GROUPS):
        q = q_ref[g, TOK:, :]
        memory_kv = kv_ref[g, TOK:, :]
        own = jnp.where(segment[0] == 0, memory_kv, read_ref[g, :MEM, :])
        attn_ref[g, :MEM, :] = attend(q, own, kv_ref[g, :TOK, :], memory_kv, TOK)
        other = jnp.where(segment[0] <= 1, memory_kv, read_ref[g, MEM:, :])
        attn_ref[g, MEM:, :] = attend(q, other, behind1_ref[g], memory_kv, TOK)
    total = project_out(row_blocks(attn_ref), out_ref, proj_ref)
    finish_rows(proj_ref, 0, MEM, total, memory_ref, post_ref, new_ref)
    finish_rows(proj_ref, MEM, MEM, total, memory_ref, post_ref, other_ref)
    project_read(other_ref, gain_ref, key_ref, value_ref, next_ref)
    lane = lax.broadcasted_iota(jnp.int32, (8, 128), 1)
    sq_ref[...] = jnp.where(lane == 0, squares_ref[...], squared_change(new_ref, previous_ref))


def last_kernel(
    segment, weight_ref, previous_ref, memory_ref, tokens_ref, squares_ref, q_ref, kv_ref,
    read_ref, post_ref, out_ref,
    tok_ref, new_ref, sq_ref,
    attn_ref, proj_ref,
):
    at_start = segment[0] == 0

    def group(g, _):
        memory_kv = kv_ref[g, TOK:, :]
        own = jnp.where(at_start, memory_kv, read_ref[g])
        attn_ref[g] = attend(q_ref[g], own, kv_ref[g, :TOK, :], memory_kv, 0)
        return 0

    lax.fori_loop(0, GROUPS, group, 0)
    total = project_out(row_blocks(attn_ref), out_ref, proj_ref)
    finish_rows(proj_ref, 0, TOK, total, tokens_ref, post_ref, tok_ref)
    finish_rows(proj_ref, TOK, MEM, total, memory_ref, post_ref, new_ref)
    lane = lax.broadcasted_iota(jnp.int32, (8, 128), 1)
    change = squared_change(new_ref, previous_ref)
    row = jnp.where(lane == 2, change, squares_ref[...]) * weight_ref[0]
    for i in range(DEVICES // 8):
        sq_ref[8 * i : 8 * (i + 1), :] = row


def whole():
    return pl.BlockSpec(memory_space=pltpu.VMEM)


def in_hbm():
    return pl.BlockSpec(memory_space=pltpu.HBM)


def in_smem():
    return pl.BlockSpec(memory_space=pltpu.SMEM)


def params(mib):
    return pltpu.CompilerParams(vmem_limit_bytes=mib * MIB)


def far(x):
    return pltpu.with_memory_space_constraint(x, pltpu.HBM)


def pinned(x):
    return pltpu.with_memory_space_constraint(x, pltpu.VMEM)


def pack(query_weight, output_weight):
    return pl.pallas_call(
        pack_kernel,
        name="pack",
        out_shape=jax.ShapeDtypeStruct((PACKED, PAIR), jnp.bfloat16),
        in_specs=[in_hbm(), in_hbm()],
        out_specs=whole(),
        scratch_shapes=[
            pltpu.VMEM((QROWS, GROUPS * PAIR), jnp.bfloat16),
            pltpu.VMEM((OROWS, WIDTH), jnp.bfloat16),
            pltpu.SemaphoreType.DMA,
            pltpu.SemaphoreType.DMA,
        ],
        compiler_params=params(2),
    )(far(query_weight), far(output_weight))


WRITTEN = jax.ShapeDtypeStruct((MEM, WIDTH), jnp.bfloat16)
SQUARES = jax.ShapeDtypeStruct((8, 128), jnp.float32)


def first_step(main, even, odd, memory, kv, behind1, behind2, gain, post_gain, segment,
               key_matrix, value_matrix, gathered):
    near = pltpu.VMEM((WIDTH, GROUPS * HEAD), jnp.bfloat16)
    sources = (main, even, odd, memory, kv, behind1, behind2)
    return pl.pallas_call(
        first_kernel,
        name="first_step",
        out_shape=(
            jax.ShapeDtypeStruct((GROUPS, ROWS, PAIR), jnp.bfloat16),
            WRITTEN,
            jax.ShapeDtypeStruct((GROUPS, 2 * MEM, PAIR), jnp.bfloat16),
            SQUARES,
            near,
            near,
            pltpu.VMEM((CHUNKS, DEVICES, OROWS, PAIR), jnp.bfloat16),
        ),
        in_specs=[in_hbm()] * 7 + [whole()] * 2 + [in_smem()] + [in_hbm()] * 3,
        out_specs=tuple(whole() for _ in range(7)),
        scratch_shapes=[pltpu.VMEM(x.shape, x.dtype) for x in sources[:4]]
        + [
            pltpu.VMEM((GROUPS, MEM, PAIR), jnp.bfloat16),
            pltpu.VMEM((3, GROUPS, TOK, PAIR), jnp.bfloat16),
            pltpu.VMEM((SLOTS, DEVICES, MAIN, PAIR), jnp.bfloat16),
            pltpu.VMEM((2, DEVICES, 2 * REST, PAIR), jnp.bfloat16),
            pltpu.VMEM((3, GROUPS, MEM, PAIR), jnp.bfloat16),
            pltpu.VMEM((CHUNKS, 3 * MEM, PAIR), jnp.float32),
            pltpu.VMEM((2 * MEM, WIDTH), jnp.bfloat16),
            pltpu.SemaphoreType.DMA((8,)),
            pltpu.SemaphoreType.DMA((GROUPS,)),
            pltpu.SemaphoreType.DMA((2,)),
            pltpu.SemaphoreType.DMA((CHUNKS,)),
            pltpu.SemaphoreType.DMA((2 * GROUPS,)),
        ],
        compiler_params=params(20),
    )(*(far(x) for x in sources), gain, post_gain, segment, far(key_matrix), far(value_matrix),
      gathered)


def middle_step(segment, previous, memory, squares, q, kv, behind1, read, gain, post_gain,
                *weights):
    return pl.pallas_call(
        middle_kernel,
        name="middle_step",
        out_shape=(
            WRITTEN,
            jax.ShapeDtypeStruct((GROUPS, MEM, PAIR), jnp.bfloat16),
            SQUARES,
        ),
        in_specs=[in_smem()] + [whole()] * (9 + len(weights)),
        out_specs=(whole(), whole(), whole()),
        scratch_shapes=[
            pltpu.VMEM((GROUPS, 2 * MEM, PAIR), jnp.bfloat16),
            pltpu.VMEM((CHUNKS, 2 * MEM, PAIR), jnp.float32),
            pltpu.VMEM((MEM, WIDTH), jnp.bfloat16),
        ],
        compiler_params=params(5),
    )(segment, previous, memory, squares, q, kv, behind1, read, gain, post_gain,
      *(pinned(x) for x in weights))


def last_step(segment, weight, previous, memory, tokens, squares, q, kv, read, post_gain,
              out_weight):
    return pl.pallas_call(
        last_kernel,
        name="last_step",
        out_shape=(
            jax.ShapeDtypeStruct((TOK, WIDTH), jnp.bfloat16),
            WRITTEN,
            jax.ShapeDtypeStruct((DEVICES, 128), jnp.float32),
        ),
        in_specs=[in_smem(), in_smem()] + [whole()] * 9,
        out_specs=(whole(), whole(), whole()),
        scratch_shapes=[
            pltpu.VMEM((GROUPS, ROWS, PAIR), jnp.bfloat16),
            pltpu.VMEM((CHUNKS, ROWS, PAIR), jnp.float32),
        ],
        compiler_params=params(10),
    )(segment, weight, previous, memory, tokens, squares, q, kv, read, post_gain,
      pinned(out_weight))


def by_head(x):
    return jnp.transpose(x.reshape(x.shape[0], GROUPS, HEAD), (1, 0, 2))


def shards(
    tokens,
    memory,
    norm_gain,
    post_gain,
    query_weight,
    key_matrix,
    value_matrix,
    output_weight,
    segment_weight,
):
    mine = pack(query_weight, output_weight)
    gathered = lax.all_gather(mine, SEG, axis=0, tiled=False)
    inputs = jnp.concatenate([tokens, memory], axis=0)
    normed = prenorm(inputs, norm_gain)
    local_k = by_head(dot(normed, key_matrix).astype(jnp.bfloat16))
    local_v = by_head(dot(normed, value_matrix).astype(jnp.bfloat16))
    kv = jnp.concatenate([local_k, local_v], axis=2)
    tokens_kv = kv[:, :TOK, :]
    behind1 = from_behind(tokens_kv, SEG, 1)
    behind2 = from_behind(tokens_kv, SEG, 2)
    by_device = normed.reshape(ROWS, DEVICES, QROWS)
    main = by_device[:, :, :MAIN].reshape(ROWS, DEVICES * MAIN)
    rest = by_device[:, :, MAIN:]
    even = jnp.pad(rest, ((0, 0), (0, 0), (0, REST))).reshape(ROWS, DEVICES * 2 * REST)
    odd = jnp.pad(rest, ((0, 0), (0, 0), (REST, 0))).reshape(ROWS, DEVICES * 2 * REST)
    post = post_gain.reshape(1, WIDTH)
    gain = norm_gain.reshape(1, WIDTH)
    segment = lax.axis_index(SEG).astype(jnp.int32).reshape(1)
    q, newest, read, squares, near_k, near_v, near_out = first_step(
        main, even, odd, memory, kv, behind1, behind2, gain, post, segment, key_matrix,
        value_matrix, gathered,
    )
    newest, read, squares = middle_step(
        segment, newest, memory, squares, q, kv, behind1, read, gain, post, near_k, near_v,
        near_out,
    )
    token_out, newest, squares = last_step(
        segment, segment_weight, newest, memory, tokens, squares, q, kv, read, post, near_out
    )
    everyone = lax.all_to_all(
        squares, SEG, split_axis=0, concat_axis=0, tiled=True
    )
    totals = jnp.sum(everyone, axis=0)[:ITERS]
    change_vec = jnp.sqrt(totals / (DEVICES * MEM * WIDTH) + eps)
    return (token_out, newest, change_vec)


def solution(mesh):
    finer = Mesh(mesh.devices.reshape(4, 4, 4, 2), SEG)
    in_specs = (P(SEG, None), P(), P(), P(), P(SEG, None), P(), P(), P(SEG, None), P(SEG))
    out_specs = (P(SEG, None), P(SEG, None), P())
    return jax.shard_map(
        shards, mesh=finer, in_specs=in_specs, out_specs=out_specs, check_vma=False
    )
```

```python
import functools

import jax
import jax.numpy as jnp
from jax import lax
from jax.experimental import pallas as pl
from jax.experimental.pallas import tpu as pltpu
from jax.sharding import Mesh
from jax.sharding import PartitionSpec as P

HEAD = 256
GROUPS = 4
PAIR = 2 * HEAD
ITERS = 3
WIDTH = 3584
MEM = 64
TOK = 256
ROWS = TOK + MEM
CHUNKS = WIDTH // PAIR
QROWS = 28
MAIN = 24
REST = QROWS - MAIN
OROWS = 16
DEVICES = 128
QBLOCK = 2 * QROWS
OFIRST = GROUPS * QROWS
PACKED = OFIRST + CHUNKS * OROWS
SEG = ("seg_0", "seg_1", "seg_2", "seg_3")
MIB = 1024 * 1024

eps = 1e-06


def from_behind(block, axis, distance):
    devices = range(lax.axis_size(axis))
    route = [(i - distance, i) for i in devices if i - distance in devices]
    return lax.ppermute(block, axis, route)


def prenorm(rows, gain):
    rows = rows.astype(jnp.float32)
    mean_sq = jnp.mean(rows * rows, axis=-1, keepdims=True)
    return (rows / jnp.sqrt(mean_sq + eps) * gain).astype(jnp.bfloat16)


def dot(a, b):
    return jnp.dot(a, b, preferred_element_type=jnp.float32)


def attend(q, read, tokens, memory, row0):
    rows = q.shape[0]
    kv = jnp.concatenate([read, tokens, memory], axis=0)
    keys = kv[:, :HEAD]
    values = kv[:, HEAD:]
    both = jnp.concatenate([q[:, :HEAD], q[:, HEAD:]], axis=0)
    score = lax.dot_general(
        both, keys, (((1,), (1,)), ((), ())), preferred_element_type=jnp.float32
    )
    row = lax.broadcasted_iota(jnp.int32, score.shape, 0)
    row = jnp.where(row >= rows, row - rows, row) + row0
    col = lax.broadcasted_iota(jnp.int32, score.shape, 1)
    expo = jnp.where(col - MEM <= row, jnp.exp(score), 0.0)
    denom = jnp.sum(expo, axis=-1, keepdims=True)
    numer = dot(expo.astype(jnp.bfloat16), values)
    attn = (numer / denom).astype(jnp.bfloat16)
    return jnp.concatenate([attn[:rows], attn[rows:]], axis=1)


def row_blocks(attn_ref):
    return jnp.concatenate([attn_ref[g] for g in range(GROUPS)], axis=1)


def project_out(attn, weight_ref, proj_ref, ready=None):
    total = jnp.zeros((attn.shape[0], 1), jnp.float32)
    for b in range(CHUNKS):
        if ready is not None:
            ready(b)
        proj = dot(attn, weight_ref[b].reshape(DEVICES * OROWS, PAIR))
        proj_ref[b] = proj
        total = total + jnp.sum(proj * proj, axis=-1, keepdims=True)
    return total


def finish_rows(proj_ref, start, count, total, residual_ref, gain_ref, out_ref, at=0):
    root = jnp.sqrt(total[start : start + count] * (1.0 / WIDTH) + eps)
    for b in range(CHUNKS):
        cols = slice(b * PAIR, (b + 1) * PAIR)
        proj = proj_ref[b, start : start + count, :]
        out = residual_ref[:, cols].astype(jnp.float32) + proj / root * gain_ref[:, cols]
        out_ref[at : at + count, cols] = out.astype(jnp.bfloat16)


def squared_change(new_ref, old_ref):
    total = jnp.zeros((MEM, PAIR), jnp.float32)
    for b in range(CHUNKS):
        cols = slice(b * PAIR, (b + 1) * PAIR)
        diff = new_ref[:, cols].astype(jnp.float32) - old_ref[:, cols].astype(jnp.float32)
        total = total + diff * diff
    return jnp.sum(total)


def pack_kernel(query_hbm, output_hbm, out_ref, query_ref, output_ref, qsem, osem):
    query_copy = pltpu.make_async_copy(query_hbm, query_ref, qsem)
    output_copy = pltpu.make_async_copy(output_hbm, output_ref, osem)
    query_copy.start()
    output_copy.start()
    query_copy.wait()
    for g in range(GROUPS):
        cols = slice(g * PAIR, (g + 1) * PAIR)
        base = (g // 2) * QBLOCK
        main = base + (g % 2) * MAIN
        rest = base + 2 * MAIN + (g % 2) * REST
        out_ref[main : main + MAIN, :] = query_ref[:MAIN, cols]
        out_ref[rest : rest + REST, :] = query_ref[MAIN:, cols]
    output_copy.wait()
    for b in range(CHUNKS):
        first = OFIRST + b * OROWS
        out_ref[first : first + OROWS, :] = output_ref[:, b * PAIR : (b + 1) * PAIR]


def project_read(new_ref, gain_ref, key_ref, value_ref, kv_ref, ready=None):
    total = jnp.zeros((new_ref.shape[0], 1), jnp.float32)
    for i in range(CHUNKS):
        rows = new_ref[:, i * PAIR : (i + 1) * PAIR].astype(jnp.float32)
        total = total + jnp.sum(rows * rows, axis=-1, keepdims=True)
    root = jnp.sqrt(total * (1.0 / WIDTH) + eps)
    for i in range(CHUNKS):
        cols = slice(i * PAIR, (i + 1) * PAIR)
        rows = new_ref[:, cols].astype(jnp.float32)
        new_ref[:, cols] = (rows / root * gain_ref[:, cols]).astype(jnp.bfloat16)
    normed = new_ref[...]
    for g in range(GROUPS):
        cols = slice(g * HEAD, (g + 1) * HEAD)
        if ready is not None:
            ready(g)
        kv_ref[g, :, :HEAD] = dot(normed, key_ref[:, cols]).astype(jnp.bfloat16)
        kv_ref[g, :, HEAD:] = dot(normed, value_ref[:, cols]).astype(jnp.bfloat16)


SLOTS = 3
SETS = 2


def first_kernel(
    main_hbm, even_hbm, odd_hbm, memory_hbm, kv_hbm, behind_hbm, gain_ref, post_ref, segment,
    key_hbm, value_hbm, gathered,
    q_ref, new_ref, read_ref, sq_ref, key_ref, value_ref, out_ref,
    main_ref, even_ref, odd_ref, memory_ref, memory_kv_ref, tokens_kv_ref,
    wmain, wrest, attn_ref, proj_ref, others_ref,
    rowsem, mainsem, restsem, outsem, kvsem,
):
    def rows_copy(i):
        source, target = (
            (main_hbm, main_ref),
            (even_hbm, even_ref),
            (odd_hbm, odd_ref),
            (kv_hbm.at[:, pl.ds(0, TOK), :], tokens_kv_ref.at[0]),
            (behind_hbm, tokens_kv_ref.at[1]),
            (kv_hbm.at[:, pl.ds(TOK, MEM), :], memory_kv_ref),
            (memory_hbm, memory_ref),
        )[i]
        return pltpu.make_async_copy(source, target, rowsem.at[i])

    def main_copy(g):
        start = (g // 2) * QBLOCK + (g % 2) * MAIN
        return pltpu.make_async_copy(
            gathered.at[:, pl.ds(start, MAIN), :], wmain.at[g % SLOTS], mainsem.at[g]
        )

    def rest_copy(i):
        start = i * QBLOCK + 2 * MAIN
        return pltpu.make_async_copy(
            gathered.at[:, pl.ds(start, 2 * REST), :], wrest.at[i], restsem.at[i]
        )

    def out_copy(b):
        return pltpu.make_async_copy(
            gathered.at[:, pl.ds(OFIRST + b * OROWS, OROWS), :], out_ref.at[b], outsem.at[b]
        )

    def kv_copy(i):
        source, target = ((key_hbm, key_ref), (value_hbm, value_ref))[i % 2]
        cols = pl.ds((i // 2) * HEAD, HEAD)
        return pltpu.make_async_copy(source.at[:, cols], target.at[:, cols], kvsem.at[i])

    waiting = [rest_copy(0), main_copy(0)] + [rows_copy(i) for i in range(3, 7)]
    waiting += [main_copy(1), rest_copy(1), main_copy(2)]
    waiting += [main_copy(3)] + [out_copy(b) for b in range(CHUNKS)] + [kv_copy(i) for i in range(2 * GROUPS)]
    waiting.reverse()

    def start(count):
        for _ in range(min(count, len(waiting))):
            waiting.pop().start()

    for i in range(3):
        rows_copy(i).start()
    start(9)
    for i in range(3):
        rows_copy(i).wait()
    for g in range(GROUPS):
        if g % 2 == 0:
            rest_copy(g // 2).wait()
        main_copy(g).wait()
        acc = dot(main_ref[...], wmain[g % SLOTS].reshape(DEVICES * MAIN, PAIR))
        rest_rows = (even_ref if g % 2 == 0 else odd_ref)[...]
        acc = acc + dot(rest_rows, wrest[g // 2].reshape(DEVICES * 2 * REST, PAIR))
        q = (acc * (1.0 / HEAD**0.5)).astype(jnp.bfloat16)
        q_ref[g] = q
        if g == 0:
            for i in range(3, 6):
                rows_copy(i).wait()
        start(3)
        memory_kv = memory_kv_ref[g]

        for i in range(SETS):
            attn_ref[i, g] = attend(q[TOK:], memory_kv, tokens_kv_ref[i, g], memory_kv, TOK)

    def out_ready(b):
        out_copy(b).wait()
        start(1)

    attn = jnp.concatenate([row_blocks(attn_ref.at[i]) for i in range(SETS)], axis=0)
    total = project_out(attn, out_ref, proj_ref, out_ready)
    start(len(waiting))
    rows_copy(6).wait()
    finish_rows(proj_ref, MEM, MEM, total, memory_ref, post_ref, others_ref)

    def kv_ready(g):
        kv_copy(2 * g).wait()
        kv_copy(2 * g + 1).wait()

    finish_rows(proj_ref, 0, MEM, total, memory_ref, post_ref, new_ref)
    sq_ref[...] = jnp.full((8, 128), squared_change(new_ref, memory_ref), jnp.float32)
    project_read(others_ref, gain_ref, key_ref, value_ref, read_ref, kv_ready)


def middle_kernel(
    segment, previous_ref, memory_ref, squares_ref, q_ref, kv_ref, read_ref,
    gain_ref, post_ref, key_ref, value_ref, out_ref,
    new_ref, next_ref, sq_ref,
    attn_ref, proj_ref, copy_ref,
):
    for g in range(GROUPS):
        memory_kv = kv_ref[g, TOK:, :]
        own = jnp.where(segment[0] == 0, memory_kv, read_ref[g])
        attn_ref[g] = attend(q_ref[g, TOK:, :], own, kv_ref[g, :TOK, :], memory_kv, TOK)
    total = project_out(row_blocks(attn_ref), out_ref, proj_ref)
    finish_rows(proj_ref, 0, MEM, total, memory_ref, post_ref, new_ref)
    copy_ref[...] = new_ref[...]
    project_read(copy_ref, gain_ref, key_ref, value_ref, next_ref)
    lane = lax.broadcasted_iota(jnp.int32, (8, 128), 1)
    sq_ref[...] = jnp.where(lane == 0, squares_ref[...], squared_change(new_ref, previous_ref))


def last_kernel(
    segment, weight_ref, previous_ref, memory_ref, tokens_ref, squares_ref, q_ref, kv_ref,
    read_ref, post_ref, out_ref,
    tok_ref, new_ref, sq_ref,
    attn_ref, proj_ref,
):
    at_start = segment[0] == 0

    def group(g, _):
        memory_kv = kv_ref[g, TOK:, :]
        own = jnp.where(at_start, memory_kv, read_ref[g])
        attn_ref[g] = attend(q_ref[g], own, kv_ref[g, :TOK, :], memory_kv, 0)
        return 0

    lax.fori_loop(0, GROUPS, group, 0, unroll=True)
    total = project_out(row_blocks(attn_ref), out_ref, proj_ref)
    finish_rows(proj_ref, 0, TOK, total, tokens_ref, post_ref, tok_ref)
    finish_rows(proj_ref, TOK, MEM, total, memory_ref, post_ref, new_ref)
    lane = lax.broadcasted_iota(jnp.int32, (8, 128), 1)
    change = squared_change(new_ref, previous_ref)
    row = jnp.where(lane == 2, change, squares_ref[...]) * weight_ref[0]
    for i in range(DEVICES // 8):
        sq_ref[8 * i : 8 * (i + 1), :] = row


def whole():
    return pl.BlockSpec(memory_space=pltpu.VMEM)


def in_hbm():
    return pl.BlockSpec(memory_space=pltpu.HBM)


def in_smem():
    return pl.BlockSpec(memory_space=pltpu.SMEM)


def params(mib):
    return pltpu.CompilerParams(vmem_limit_bytes=mib * MIB)


def far(x):
    return pltpu.with_memory_space_constraint(x, pltpu.HBM)


def pinned(x):
    return pltpu.with_memory_space_constraint(x, pltpu.VMEM)


def pack(query_weight, output_weight):
    return pl.pallas_call(
        pack_kernel,
        name="pack",
        out_shape=jax.ShapeDtypeStruct((PACKED, PAIR), jnp.bfloat16),
        in_specs=[in_hbm(), in_hbm()],
        out_specs=whole(),
        scratch_shapes=[
            pltpu.VMEM((QROWS, GROUPS * PAIR), jnp.bfloat16),
            pltpu.VMEM((OROWS, WIDTH), jnp.bfloat16),
            pltpu.SemaphoreType.DMA,
            pltpu.SemaphoreType.DMA,
        ],
        compiler_params=params(2),
    )(far(query_weight), far(output_weight))


WRITTEN = jax.ShapeDtypeStruct((MEM, WIDTH), jnp.bfloat16)
SQUARES = jax.ShapeDtypeStruct((8, 128), jnp.float32)


def first_step(main, even, odd, memory, kv, behind, gain, post_gain, segment,
               key_matrix, value_matrix, gathered):
    near = pltpu.VMEM((WIDTH, GROUPS * HEAD), jnp.bfloat16)
    sources = (main, even, odd, memory, kv, behind)
    return pl.pallas_call(
        first_kernel,
        name="first_step",
        out_shape=(
            jax.ShapeDtypeStruct((GROUPS, ROWS, PAIR), jnp.bfloat16),
            WRITTEN,
            jax.ShapeDtypeStruct((GROUPS, MEM, PAIR), jnp.bfloat16),
            SQUARES,
            near,
            near,
            pltpu.VMEM((CHUNKS, DEVICES, OROWS, PAIR), jnp.bfloat16),
        ),
        in_specs=[in_hbm()] * 6 + [whole()] * 2 + [in_smem()] + [in_hbm()] * 3,
        out_specs=tuple(whole() for _ in range(7)),
        scratch_shapes=[pltpu.VMEM(x.shape, x.dtype) for x in sources[:4]]
        + [
            pltpu.VMEM((GROUPS, MEM, PAIR), jnp.bfloat16),
            pltpu.VMEM((SETS, GROUPS, TOK, PAIR), jnp.bfloat16),
            pltpu.VMEM((SLOTS, DEVICES, MAIN, PAIR), jnp.bfloat16),
            pltpu.VMEM((2, DEVICES, 2 * REST, PAIR), jnp.bfloat16),
            pltpu.VMEM((SETS, GROUPS, MEM, PAIR), jnp.bfloat16),
            pltpu.VMEM((CHUNKS, SETS * MEM, PAIR), jnp.float32),
            pltpu.VMEM((MEM, WIDTH), jnp.bfloat16),
            pltpu.SemaphoreType.DMA((7,)),
            pltpu.SemaphoreType.DMA((GROUPS,)),
            pltpu.SemaphoreType.DMA((2,)),
            pltpu.SemaphoreType.DMA((CHUNKS,)),
            pltpu.SemaphoreType.DMA((2 * GROUPS,)),
        ],
        compiler_params=params(20),
    )(*(far(x) for x in sources), gain, post_gain, segment, far(key_matrix), far(value_matrix),
      gathered)


def middle_step(segment, previous, memory, squares, q, kv, read, gain, post_gain,
                *weights):
    return pl.pallas_call(
        middle_kernel,
        name="middle_step",
        out_shape=(
            WRITTEN,
            jax.ShapeDtypeStruct((GROUPS, MEM, PAIR), jnp.bfloat16),
            SQUARES,
        ),
        in_specs=[in_smem()] + [whole()] * (8 + len(weights)),
        out_specs=(whole(), whole(), whole()),
        scratch_shapes=[
            pltpu.VMEM((GROUPS, MEM, PAIR), jnp.bfloat16),
            pltpu.VMEM((CHUNKS, MEM, PAIR), jnp.float32),
            pltpu.VMEM((MEM, WIDTH), jnp.bfloat16),
        ],
        compiler_params=params(5),
    )(segment, previous, memory, squares, q, kv, read, gain, post_gain,
      *(pinned(x) for x in weights))


def last_step(segment, weight, previous, memory, tokens, squares, q, kv, read, post_gain,
              out_weight):
    return pl.pallas_call(
        last_kernel,
        name="last_step",
        out_shape=(
            jax.ShapeDtypeStruct((TOK, WIDTH), jnp.bfloat16),
            WRITTEN,
            jax.ShapeDtypeStruct((DEVICES, 128), jnp.float32),
        ),
        in_specs=[in_smem(), in_smem()] + [whole()] * 9,
        out_specs=(whole(), whole(), whole()),
        scratch_shapes=[
            pltpu.VMEM((GROUPS, ROWS, PAIR), jnp.bfloat16),
            pltpu.VMEM((CHUNKS, ROWS, PAIR), jnp.float32),
        ],
        compiler_params=params(10),
    )(segment, weight, previous, memory, tokens, squares, q, kv, read, post_gain,
      pinned(out_weight))


def by_head(x):
    return jnp.transpose(x.reshape(x.shape[0], GROUPS, HEAD), (1, 0, 2))


def shards(
    tokens,
    memory,
    norm_gain,
    post_gain,
    query_weight,
    key_matrix,
    value_matrix,
    output_weight,
    segment_weight,
):
    mine = pack(query_weight, output_weight)
    gathered = lax.all_gather(mine, SEG, axis=0, tiled=False)
    inputs = jnp.concatenate([tokens, memory], axis=0)
    normed = prenorm(inputs, norm_gain)
    local_k = by_head(dot(normed, key_matrix).astype(jnp.bfloat16))
    local_v = by_head(dot(normed, value_matrix).astype(jnp.bfloat16))
    kv = jnp.concatenate([local_k, local_v], axis=2)
    tokens_kv = kv[:, :TOK, :]
    behind = from_behind(tokens_kv, SEG, 1)
    by_device = normed.reshape(ROWS, DEVICES, QROWS)
    main = by_device[:, :, :MAIN].reshape(ROWS, DEVICES * MAIN)
    rest = by_device[:, :, MAIN:]
    even = jnp.pad(rest, ((0, 0), (0, 0), (0, REST))).reshape(ROWS, DEVICES * 2 * REST)
    odd = jnp.pad(rest, ((0, 0), (0, 0), (REST, 0))).reshape(ROWS, DEVICES * 2 * REST)
    post = post_gain.reshape(1, WIDTH)
    gain = norm_gain.reshape(1, WIDTH)
    segment = lax.axis_index(SEG).astype(jnp.int32).reshape(1)
    q, newest, read, squares, near_k, near_v, near_out = first_step(
        main, even, odd, memory, kv, behind, gain, post, segment, key_matrix,
        value_matrix, gathered,
    )
    newest, read, squares = middle_step(
        segment, newest, memory, squares, q, kv, read, gain, post, near_k, near_v, near_out
    )
    read = from_behind(read, SEG, 1)
    token_out, newest, squares = last_step(
        segment, segment_weight, newest, memory, tokens, squares, q, kv, read, post, near_out
    )
    everyone = lax.all_to_all(
        squares, SEG, split_axis=0, concat_axis=0, tiled=True
    )
    totals = jnp.sum(everyone, axis=0)[:ITERS]
    change_vec = jnp.sqrt(totals / (DEVICES * MEM * WIDTH) + eps)
    return (token_out, newest, change_vec)


def solution(mesh):
    finer = Mesh(mesh.devices.reshape(4, 4, 4, 2), SEG)
    in_specs = (P(SEG, None), P(), P(), P(), P(SEG, None), P(), P(), P(SEG, None), P(SEG))
    out_specs = (P(SEG, None), P(SEG, None), P())
    return jax.shard_map(
        shards, mesh=finer, in_specs=in_specs, out_specs=out_specs, check_vma=False
    )
```

```python
import functools

import jax
import jax.numpy as jnp
from jax import lax
from jax.experimental import pallas as pl
from jax.experimental.pallas import tpu as pltpu
from jax.sharding import Mesh
from jax.sharding import PartitionSpec as P

HEAD = 256
GROUPS = 4
PAIR = 2 * HEAD
ITERS = 3
WIDTH = 3584
MEM = 64
TOK = 256
ROWS = TOK + MEM
CHUNKS = WIDTH // PAIR
QROWS = 28
MAIN = 24
REST = QROWS - MAIN
OROWS = 16
DEVICES = 128
QBLOCK = 2 * QROWS
OFIRST = GROUPS * QROWS
PACKED = OFIRST + CHUNKS * OROWS
SEG = ("seg_0", "seg_1", "seg_2", "seg_3")
MIB = 1024 * 1024

eps = 1e-06


def from_behind(block, axis, distance):
    devices = range(lax.axis_size(axis))
    route = [(i - distance, i) for i in devices if i - distance in devices]
    return lax.ppermute(block, axis, route)


def prenorm(rows, gain):
    rows = rows.astype(jnp.float32)
    mean_sq = jnp.mean(rows * rows, axis=-1, keepdims=True)
    return (rows / jnp.sqrt(mean_sq + eps) * gain).astype(jnp.bfloat16)


def dot(a, b):
    return jnp.dot(a, b, preferred_element_type=jnp.float32)


def attend(q, read, tokens, memory, row0):
    rows = q.shape[0]
    kv = jnp.concatenate([read, tokens, memory], axis=0)
    keys = kv[:, :HEAD]
    values = kv[:, HEAD:]
    both = jnp.concatenate([q[:, :HEAD], q[:, HEAD:]], axis=0)
    score = lax.dot_general(
        both, keys, (((1,), (1,)), ((), ())), preferred_element_type=jnp.float32
    )
    row = lax.broadcasted_iota(jnp.int32, score.shape, 0)
    row = jnp.where(row >= rows, row - rows, row) + row0
    col = lax.broadcasted_iota(jnp.int32, score.shape, 1)
    expo = jnp.where(col - MEM <= row, jnp.exp(score), 0.0)
    denom = jnp.sum(expo, axis=-1, keepdims=True)
    numer = dot(expo.astype(jnp.bfloat16), values)
    attn = (numer / denom).astype(jnp.bfloat16)
    return jnp.concatenate([attn[:rows], attn[rows:]], axis=1)


def row_blocks(attn_ref):
    return jnp.concatenate([attn_ref[g] for g in range(GROUPS)], axis=1)


def project_out(attn, weight_ref, proj_ref, ready=None):
    total = jnp.zeros((attn.shape[0], 1), jnp.float32)
    for b in range(CHUNKS):
        if ready is not None:
            ready(b)
        proj = dot(attn, weight_ref[b].reshape(DEVICES * OROWS, PAIR))
        proj_ref[b] = proj
        total = total + jnp.sum(proj * proj, axis=-1, keepdims=True)
    return total


def finish_rows(proj_ref, start, count, total, residual_ref, gain_ref, out_ref, at=0):
    root = jnp.sqrt(total[start : start + count] * (1.0 / WIDTH) + eps)
    for b in range(CHUNKS):
        cols = slice(b * PAIR, (b + 1) * PAIR)
        proj = proj_ref[b, start : start + count, :]
        out = residual_ref[:, cols].astype(jnp.float32) + proj / root * gain_ref[:, cols]
        out_ref[at : at + count, cols] = out.astype(jnp.bfloat16)


def squared_change(new_ref, old_ref):
    total = jnp.zeros((MEM, PAIR), jnp.float32)
    for b in range(CHUNKS):
        cols = slice(b * PAIR, (b + 1) * PAIR)
        diff = new_ref[:, cols].astype(jnp.float32) - old_ref[:, cols].astype(jnp.float32)
        total = total + diff * diff
    return jnp.sum(total)


def pack_kernel(query_hbm, output_hbm, out_ref, query_ref, output_ref, qsem, osem):
    query_copy = pltpu.make_async_copy(query_hbm, query_ref, qsem)
    output_copy = pltpu.make_async_copy(output_hbm, output_ref, osem)
    query_copy.start()
    output_copy.start()
    query_copy.wait()
    for g in range(GROUPS):
        cols = slice(g * PAIR, (g + 1) * PAIR)
        base = (g // 2) * QBLOCK
        main = base + (g % 2) * MAIN
        rest = base + 2 * MAIN + (g % 2) * REST
        out_ref[main : main + MAIN, :] = query_ref[:MAIN, cols]
        out_ref[rest : rest + REST, :] = query_ref[MAIN:, cols]
    output_copy.wait()
    for b in range(CHUNKS):
        first = OFIRST + b * OROWS
        out_ref[first : first + OROWS, :] = output_ref[:, b * PAIR : (b + 1) * PAIR]


def project_read(new_ref, gain_ref, key_ref, value_ref, kv_ref, ready=None):
    total = jnp.zeros((new_ref.shape[0], 1), jnp.float32)
    for i in range(CHUNKS):
        rows = new_ref[:, i * PAIR : (i + 1) * PAIR].astype(jnp.float32)
        total = total + jnp.sum(rows * rows, axis=-1, keepdims=True)
    root = jnp.sqrt(total * (1.0 / WIDTH) + eps)
    for i in range(CHUNKS):
        cols = slice(i * PAIR, (i + 1) * PAIR)
        rows = new_ref[:, cols].astype(jnp.float32)
        new_ref[:, cols] = (rows / root * gain_ref[:, cols]).astype(jnp.bfloat16)
    normed = new_ref[...]
    for g in range(GROUPS):
        cols = slice(g * HEAD, (g + 1) * HEAD)
        if ready is not None:
            ready(g)
        kv_ref[g, :, :HEAD] = dot(normed, key_ref[:, cols]).astype(jnp.bfloat16)
        kv_ref[g, :, HEAD:] = dot(normed, value_ref[:, cols]).astype(jnp.bfloat16)


SLOTS = 2
SETS = 3


def first_kernel(
    main_hbm, even_hbm, odd_hbm, memory_hbm, kv_hbm, behind1_hbm, behind2_hbm, gain_ref, post_ref,
    segment, key_hbm, value_hbm, gathered,
    q_ref, new_ref, read_ref, sq_ref, key_ref, value_ref, out_ref,
    main_ref, even_ref, odd_ref, memory_ref, memory_kv_ref, tokens_kv_ref,
    wmain, wrest, attn_ref, proj_ref, others_ref,
    rowsem, mainsem, restsem, outsem, kvsem,
):
    def rows_copy(i):
        source, target = (
            (main_hbm, main_ref),
            (even_hbm, even_ref),
            (odd_hbm, odd_ref),
            (kv_hbm.at[:, pl.ds(0, TOK), :], tokens_kv_ref.at[0]),
            (behind1_hbm, tokens_kv_ref.at[1]),
            (behind2_hbm, tokens_kv_ref.at[2]),
            (kv_hbm.at[:, pl.ds(TOK, MEM), :], memory_kv_ref),
            (memory_hbm, memory_ref),
        )[i]
        return pltpu.make_async_copy(source, target, rowsem.at[i])

    def main_copy(g):
        start = (g // 2) * QBLOCK + (g % 2) * MAIN
        return pltpu.make_async_copy(
            gathered.at[:, pl.ds(start, MAIN), :], wmain.at[g % SLOTS], mainsem.at[g]
        )

    def rest_copy(i):
        start = i * QBLOCK + 2 * MAIN
        return pltpu.make_async_copy(
            gathered.at[:, pl.ds(start, 2 * REST), :], wrest.at[i], restsem.at[i]
        )

    def out_copy(b):
        return pltpu.make_async_copy(
            gathered.at[:, pl.ds(OFIRST + b * OROWS, OROWS), :], out_ref.at[b], outsem.at[b]
        )

    def kv_copy(i):
        source, target = ((key_hbm, key_ref), (value_hbm, value_ref))[i % 2]
        cols = pl.ds((i // 2) * HEAD, HEAD)
        return pltpu.make_async_copy(source.at[:, cols], target.at[:, cols], kvsem.at[i])

    waiting = [rest_copy(0), main_copy(0)] + [rows_copy(i) for i in range(3, 8)]
    waiting += [main_copy(1), rest_copy(1)]
    waiting += [main_copy(2), out_copy(0), out_copy(1)]
    waiting += [main_copy(3)] + [out_copy(b) for b in range(2, CHUNKS)] + [kv_copy(i) for i in range(2 * GROUPS)]
    waiting.reverse()

    def start(count):
        for _ in range(min(count, len(waiting))):
            waiting.pop().start()

    for i in range(3):
        rows_copy(i).start()
    start(9)
    for i in range(3):
        rows_copy(i).wait()
    for g in range(GROUPS):
        if g % 2 == 0:
            rest_copy(g // 2).wait()
        main_copy(g).wait()
        acc = dot(main_ref[...], wmain[g % SLOTS].reshape(DEVICES * MAIN, PAIR))
        rest_rows = (even_ref if g % 2 == 0 else odd_ref)[...]
        acc = acc + dot(rest_rows, wrest[g // 2].reshape(DEVICES * 2 * REST, PAIR))
        q = (acc * (1.0 / HEAD**0.5)).astype(jnp.bfloat16)
        q_ref[g] = q
        if g == 0:
            for i in range(3, 7):
                rows_copy(i).wait()
        start(3)
        memory_kv = memory_kv_ref[g]


        def segments(i, _):
            attn_ref[i, g] = attend(q_ref[g, TOK:, :], memory_kv_ref[g], tokens_kv_ref[i, g],
                                    memory_kv_ref[g], TOK)
            return 0

        attn_ref[0, g] = attend(q[TOK:], memory_kv, tokens_kv_ref[0, g], memory_kv, TOK)
        lax.fori_loop(1, SETS, segments, 0)

    def out_ready(b):
        out_copy(b).wait()
        start(1)

    attn = jnp.concatenate([row_blocks(attn_ref.at[i]) for i in range(SETS)], axis=0)
    total = project_out(attn, out_ref, proj_ref, out_ready)
    start(len(waiting))
    rows_copy(7).wait()
    for i in range(1, SETS):
        finish_rows(
            proj_ref, i * MEM, MEM, total, memory_ref, post_ref, others_ref, (i - 1) * MEM
        )

    def kv_ready(g):
        kv_copy(2 * g).wait()
        kv_copy(2 * g + 1).wait()

    finish_rows(proj_ref, 0, MEM, total, memory_ref, post_ref, new_ref)
    sq_ref[...] = jnp.full((8, 128), squared_change(new_ref, memory_ref), jnp.float32)
    project_read(others_ref, gain_ref, key_ref, value_ref, read_ref, kv_ready)


def middle_kernel(
    segment, previous_ref, memory_ref, squares_ref, q_ref, read_ref,
    gain_ref, post_ref, kv_hbm, behind_hbm, key_ref, value_ref, out_ref,
    new_ref, next_ref, sq_ref,
    attn_ref, proj_ref, other_ref, kv_ref, behind_ref, sem,
):
    kv_copy = pltpu.make_async_copy(kv_hbm, kv_ref, sem.at[0])
    behind_copy = pltpu.make_async_copy(behind_hbm, behind_ref, sem.at[1])
    kv_copy.start()
    behind_copy.start()
    kv_copy.wait()
    behind_copy.wait()
    at_start = segment[0] == 0
    near_start = segment[0] <= 1

    def group(g, _):
        q = q_ref[g, TOK:, :]
        memory_kv = kv_ref[g, TOK:, :]
        own = jnp.where(at_start, memory_kv, read_ref[g, :MEM, :])
        other = jnp.where(near_start, memory_kv, read_ref[g, MEM:, :])
        attn_ref[g, :MEM, :] = attend(q, own, kv_ref[g, :TOK, :], memory_kv, TOK)
        attn_ref[g, MEM:, :] = attend(q, other, behind_ref[g], memory_kv, TOK)
        return 0

    lax.fori_loop(0, GROUPS, group, 0)
    total = project_out(row_blocks(attn_ref), out_ref, proj_ref)
    finish_rows(proj_ref, 0, MEM, total, memory_ref, post_ref, new_ref)
    finish_rows(proj_ref, MEM, MEM, total, memory_ref, post_ref, other_ref)
    project_read(other_ref, gain_ref, key_ref, value_ref, next_ref)
    lane = lax.broadcasted_iota(jnp.int32, (8, 128), 1)
    sq_ref[...] = jnp.where(lane == 0, squares_ref[...], squared_change(new_ref, previous_ref))


def last_kernel(
    segment, weight_ref, previous_ref, memory_ref, tokens_ref, squares_ref, q_ref, kv_ref,
    read_ref, post_ref, out_ref,
    tok_ref, new_ref, sq_ref,
    attn_ref, proj_ref,
):
    at_start = segment[0] == 0

    def group(g, _):
        memory_kv = kv_ref[g, TOK:, :]
        own = jnp.where(at_start, memory_kv, read_ref[g])
        attn_ref[g] = attend(q_ref[g], own, kv_ref[g, :TOK, :], memory_kv, 0)
        return 0

    lax.fori_loop(0, GROUPS, group, 0, unroll=True)
    total = project_out(row_blocks(attn_ref), out_ref, proj_ref)
    finish_rows(proj_ref, 0, TOK, total, tokens_ref, post_ref, tok_ref)
    finish_rows(proj_ref, TOK, MEM, total, memory_ref, post_ref, new_ref)
    lane = lax.broadcasted_iota(jnp.int32, (8, 128), 1)
    change = squared_change(new_ref, previous_ref)
    row = jnp.where(lane == 2, change, squares_ref[...]) * weight_ref[0]
    for i in range(DEVICES // 8):
        sq_ref[8 * i : 8 * (i + 1), :] = row


def whole():
    return pl.BlockSpec(memory_space=pltpu.VMEM)


def in_hbm():
    return pl.BlockSpec(memory_space=pltpu.HBM)


def in_smem():
    return pl.BlockSpec(memory_space=pltpu.SMEM)


def params(mib):
    return pltpu.CompilerParams(vmem_limit_bytes=mib * MIB)


def far(x):
    return pltpu.with_memory_space_constraint(x, pltpu.HBM)


def pinned(x):
    return pltpu.with_memory_space_constraint(x, pltpu.VMEM)


def pack(query_weight, output_weight):
    return pl.pallas_call(
        pack_kernel,
        name="pack",
        out_shape=jax.ShapeDtypeStruct((PACKED, PAIR), jnp.bfloat16),
        in_specs=[in_hbm(), in_hbm()],
        out_specs=whole(),
        scratch_shapes=[
            pltpu.VMEM((QROWS, GROUPS * PAIR), jnp.bfloat16),
            pltpu.VMEM((OROWS, WIDTH), jnp.bfloat16),
            pltpu.SemaphoreType.DMA,
            pltpu.SemaphoreType.DMA,
        ],
        compiler_params=params(2),
    )(far(query_weight), far(output_weight))


WRITTEN = jax.ShapeDtypeStruct((MEM, WIDTH), jnp.bfloat16)
SQUARES = jax.ShapeDtypeStruct((8, 128), jnp.float32)


def first_step(main, even, odd, memory, kv, behind1, behind2, gain, post_gain, segment,
               key_matrix, value_matrix, gathered):
    near = pltpu.VMEM((WIDTH, GROUPS * HEAD), jnp.bfloat16)
    sources = (main, even, odd, memory, kv, behind1, behind2)
    return pl.pallas_call(
        first_kernel,
        name="first_step",
        out_shape=(
            jax.ShapeDtypeStruct((GROUPS, ROWS, PAIR), jnp.bfloat16),
            WRITTEN,
            jax.ShapeDtypeStruct((GROUPS, 2 * MEM, PAIR), jnp.bfloat16),
            SQUARES,
            near,
            near,
            pltpu.VMEM((CHUNKS, DEVICES, OROWS, PAIR), jnp.bfloat16),
        ),
        in_specs=[in_hbm()] * 7 + [whole()] * 2 + [in_smem()] + [in_hbm()] * 3,
        out_specs=tuple(whole() for _ in range(7)),
        scratch_shapes=[pltpu.VMEM(x.shape, x.dtype) for x in sources[:4]]
        + [
            pltpu.VMEM((GROUPS, MEM, PAIR), jnp.bfloat16),
            pltpu.VMEM((SETS, GROUPS, TOK, PAIR), jnp.bfloat16),
            pltpu.VMEM((SLOTS, DEVICES, MAIN, PAIR), jnp.bfloat16),
            pltpu.VMEM((2, DEVICES, 2 * REST, PAIR), jnp.bfloat16),
            pltpu.VMEM((SETS, GROUPS, MEM, PAIR), jnp.bfloat16),
            pltpu.VMEM((CHUNKS, SETS * MEM, PAIR), jnp.float32),
            pltpu.VMEM((2 * MEM, WIDTH), jnp.bfloat16),
            pltpu.SemaphoreType.DMA((8,)),
            pltpu.SemaphoreType.DMA((GROUPS,)),
            pltpu.SemaphoreType.DMA((2,)),
            pltpu.SemaphoreType.DMA((CHUNKS,)),
            pltpu.SemaphoreType.DMA((2 * GROUPS,)),
        ],
        compiler_params=params(19),
    )(*(far(x) for x in sources), gain, post_gain, segment, far(key_matrix), far(value_matrix),
      gathered)


def middle_step(segment, previous, memory, squares, q, kv, read, gain, post_gain, behind,
                *weights):
    return pl.pallas_call(
        middle_kernel,
        name="middle_step",
        out_shape=(
            WRITTEN,
            jax.ShapeDtypeStruct((GROUPS, MEM, PAIR), jnp.bfloat16),
            SQUARES,
        ),
        in_specs=[in_smem()] + [whole()] * 7 + [in_hbm()] * 2 + [whole()] * len(weights),
        out_specs=(whole(), whole(), whole()),
        scratch_shapes=[
            pltpu.VMEM((GROUPS, 2 * MEM, PAIR), jnp.bfloat16),
            pltpu.VMEM((CHUNKS, 2 * MEM, PAIR), jnp.float32),
            pltpu.VMEM((MEM, WIDTH), jnp.bfloat16),
            pltpu.VMEM((GROUPS, ROWS, PAIR), jnp.bfloat16),
            pltpu.VMEM((GROUPS, TOK, PAIR), jnp.bfloat16),
            pltpu.SemaphoreType.DMA((2,)),
        ],
        compiler_params=params(7),
    )(segment, previous, memory, squares, q, read, gain, post_gain,
      far(kv), far(behind), *(pinned(x) for x in weights))


def last_step(segment, weight, previous, memory, tokens, squares, q, kv, read, post_gain,
              out_weight):
    return pl.pallas_call(
        last_kernel,
        name="last_step",
        out_shape=(
            jax.ShapeDtypeStruct((TOK, WIDTH), jnp.bfloat16),
            WRITTEN,
            jax.ShapeDtypeStruct((DEVICES, 128), jnp.float32),
        ),
        in_specs=[in_smem(), in_smem()] + [whole()] * 9,
        out_specs=(whole(), whole(), whole()),
        scratch_shapes=[
            pltpu.VMEM((GROUPS, ROWS, PAIR), jnp.bfloat16),
            pltpu.VMEM((CHUNKS, ROWS, PAIR), jnp.float32),
        ],
        compiler_params=params(10),
    )(segment, weight, previous, memory, tokens, squares, q, kv, read, post_gain,
      pinned(out_weight))


def by_head(x):
    return jnp.transpose(x.reshape(x.shape[0], GROUPS, HEAD), (1, 0, 2))


def shards(
    tokens,
    memory,
    norm_gain,
    post_gain,
    query_weight,
    key_matrix,
    value_matrix,
    output_weight,
    segment_weight,
):
    mine = pack(query_weight, output_weight)
    gathered = lax.all_gather(mine, SEG, axis=0, tiled=False)
    inputs = jnp.concatenate([tokens, memory], axis=0)
    normed = prenorm(inputs, norm_gain)
    local_k = by_head(dot(normed, key_matrix).astype(jnp.bfloat16))
    local_v = by_head(dot(normed, value_matrix).astype(jnp.bfloat16))
    kv = jnp.concatenate([local_k, local_v], axis=2)
    tokens_kv = kv[:, :TOK, :]
    behind1 = from_behind(tokens_kv, SEG, 1)
    behind2 = from_behind(behind1, SEG, 1)
    by_device = normed.reshape(ROWS, DEVICES, QROWS)
    main = by_device[:, :, :MAIN].reshape(ROWS, DEVICES * MAIN)
    rest = by_device[:, :, MAIN:]
    even = jnp.pad(rest, ((0, 0), (0, 0), (0, REST))).reshape(ROWS, DEVICES * 2 * REST)
    odd = jnp.pad(rest, ((0, 0), (0, 0), (REST, 0))).reshape(ROWS, DEVICES * 2 * REST)
    post = post_gain.reshape(1, WIDTH)
    gain = norm_gain.reshape(1, WIDTH)
    segment = lax.axis_index(SEG).astype(jnp.int32).reshape(1)
    q, newest, read, squares, near_k, near_v, near_out = first_step(
        main, even, odd, memory, kv, behind1, behind2, gain, post, segment, key_matrix,
        value_matrix, gathered,
    )
    newest, read, squares = middle_step(
        segment, newest, memory, squares, q, kv, read, gain, post, behind1, near_k, near_v,
        near_out,
    )
    token_out, newest, squares = last_step(
        segment, segment_weight, newest, memory, tokens, squares, q, kv, read, post, near_out
    )
    everyone = lax.all_to_all(
        squares, SEG, split_axis=0, concat_axis=0, tiled=True
    )
    totals = jnp.sum(everyone, axis=0)[:ITERS]
    change_vec = jnp.sqrt(totals / (DEVICES * MEM * WIDTH) + eps)
    return (token_out, newest, change_vec)


def solution(mesh):
    finer = Mesh(mesh.devices.reshape(4, 4, 4, 2), SEG)
    in_specs = (P(SEG, None), P(), P(), P(), P(SEG, None), P(), P(), P(SEG, None), P(SEG))
    out_specs = (P(SEG, None), P(SEG, None), P())
    return jax.shard_map(
        shards, mesh=finer, in_specs=in_specs, out_specs=out_specs, check_vma=False
    )
```

```python
import functools

import jax
import jax.numpy as jnp
from jax import lax
from jax.experimental import pallas as pl
from jax.experimental.pallas import tpu as pltpu
from jax.sharding import Mesh
from jax.sharding import PartitionSpec as P

HEAD = 256
GROUPS = 4
PAIR = 2 * HEAD
ITERS = 3
WIDTH = 3584
MEM = 64
TOK = 256
ROWS = TOK + MEM
CHUNKS = WIDTH // PAIR
QROWS = 28
MAIN = 24
REST = QROWS - MAIN
OROWS = 16
DEVICES = 128
QBLOCK = 2 * QROWS
OFIRST = GROUPS * QROWS
PACKED = OFIRST + CHUNKS * OROWS
SEG = ("seg_0", "seg_1", "seg_2", "seg_3")
MIB = 1024 * 1024

eps = 1e-06


def from_behind(block, axis, distance):
    devices = range(lax.axis_size(axis))
    route = [(i - distance, i) for i in devices if i - distance in devices]
    return lax.ppermute(block, axis, route)


def prenorm(rows, gain):
    rows = rows.astype(jnp.float32)
    mean_sq = jnp.mean(rows * rows, axis=-1, keepdims=True)
    return (rows / jnp.sqrt(mean_sq + eps) * gain).astype(jnp.bfloat16)


def dot(a, b):
    return jnp.dot(a, b, preferred_element_type=jnp.float32)


def attend(q, read, tokens, memory, row0):
    rows = q.shape[0]
    kv = jnp.concatenate([read, tokens, memory], axis=0)
    keys = kv[:, :HEAD]
    values = kv[:, HEAD:]
    both = jnp.concatenate([q[:, :HEAD], q[:, HEAD:]], axis=0)
    score = lax.dot_general(
        both, keys, (((1,), (1,)), ((), ())), preferred_element_type=jnp.float32
    )
    row = lax.broadcasted_iota(jnp.int32, score.shape, 0)
    row = jnp.where(row >= rows, row - rows, row) + row0
    col = lax.broadcasted_iota(jnp.int32, score.shape, 1)
    expo = jnp.where(col - MEM <= row, jnp.exp(score), 0.0)
    denom = jnp.sum(expo, axis=-1, keepdims=True)
    numer = dot(expo.astype(jnp.bfloat16), values)
    attn = (numer / denom).astype(jnp.bfloat16)
    return jnp.concatenate([attn[:rows], attn[rows:]], axis=1)


def row_blocks(attn_ref):
    return jnp.concatenate([attn_ref[g] for g in range(GROUPS)], axis=1)


def project_out(attn, weight_ref, proj_ref, ready=None):
    total = jnp.zeros((attn.shape[0], 1), jnp.float32)
    for b in range(CHUNKS):
        if ready is not None:
            ready(b)
        proj = dot(attn, weight_ref[b].reshape(DEVICES * OROWS, PAIR))
        proj_ref[b] = proj
        total = total + jnp.sum(proj * proj, axis=-1, keepdims=True)
    return total


def finish_rows(proj_ref, start, count, total, residual_ref, gain_ref, out_ref, at=0):
    root = jnp.sqrt(total[start : start + count] * (1.0 / WIDTH) + eps)
    for b in range(CHUNKS):
        cols = slice(b * PAIR, (b + 1) * PAIR)
        proj = proj_ref[b, start : start + count, :]
        out = residual_ref[:, cols].astype(jnp.float32) + proj / root * gain_ref[:, cols]
        out_ref[at : at + count, cols] = out.astype(jnp.bfloat16)


def squared_change(new_ref, old_ref):
    total = jnp.zeros((MEM, PAIR), jnp.float32)
    for b in range(CHUNKS):
        cols = slice(b * PAIR, (b + 1) * PAIR)
        diff = new_ref[:, cols].astype(jnp.float32) - old_ref[:, cols].astype(jnp.float32)
        total = total + diff * diff
    return jnp.sum(total)


def pack_kernel(query_hbm, output_hbm, out_ref, query_ref, output_ref, qsem, osem):
    query_copy = pltpu.make_async_copy(query_hbm, query_ref, qsem)
    output_copy = pltpu.make_async_copy(output_hbm, output_ref, osem)
    query_copy.start()
    output_copy.start()
    query_copy.wait()
    for g in range(GROUPS):
        cols = slice(g * PAIR, (g + 1) * PAIR)
        base = (g // 2) * QBLOCK
        main = base + (g % 2) * MAIN
        rest = base + 2 * MAIN + (g % 2) * REST
        out_ref[main : main + MAIN, :] = query_ref[:MAIN, cols]
        out_ref[rest : rest + REST, :] = query_ref[MAIN:, cols]
    output_copy.wait()
    for b in range(CHUNKS):
        first = OFIRST + b * OROWS
        out_ref[first : first + OROWS, :] = output_ref[:, b * PAIR : (b + 1) * PAIR]


def project_read(new_ref, gain_ref, key_ref, value_ref, kv_ref, ready=None):
    total = jnp.zeros((new_ref.shape[0], 1), jnp.float32)
    for i in range(CHUNKS):
        rows = new_ref[:, i * PAIR : (i + 1) * PAIR].astype(jnp.float32)
        total = total + jnp.sum(rows * rows, axis=-1, keepdims=True)
    root = jnp.sqrt(total * (1.0 / WIDTH) + eps)
    for i in range(CHUNKS):
        cols = slice(i * PAIR, (i + 1) * PAIR)
        rows = new_ref[:, cols].astype(jnp.float32)
        new_ref[:, cols] = (rows / root * gain_ref[:, cols]).astype(jnp.bfloat16)
    normed = new_ref[...]
    for g in range(GROUPS):
        cols = slice(g * HEAD, (g + 1) * HEAD)
        if ready is not None:
            ready(g)
        kv_ref[g, :, :HEAD] = dot(normed, key_ref[:, cols]).astype(jnp.bfloat16)
        kv_ref[g, :, HEAD:] = dot(normed, value_ref[:, cols]).astype(jnp.bfloat16)


SLOTS = 3
SETS = 2


def first_kernel(
    main_hbm, even_hbm, odd_hbm, memory_hbm, kv_hbm, behind_hbm, gain_ref, post_ref, segment,
    key_hbm, value_hbm, gathered,
    q_ref, new_ref, read_ref, sq_ref, key_ref, value_ref, out_ref,
    main_ref, even_ref, odd_ref, memory_ref, memory_kv_ref, tokens_kv_ref,
    wmain, wrest, attn_ref, proj_ref, others_ref,
    rowsem, mainsem, restsem, outsem, kvsem,
):
    def rows_copy(i):
        source, target = (
            (main_hbm, main_ref),
            (even_hbm, even_ref),
            (odd_hbm, odd_ref),
            (kv_hbm.at[:, pl.ds(0, TOK), :], tokens_kv_ref.at[0]),
            (behind_hbm, tokens_kv_ref.at[1]),
            (kv_hbm.at[:, pl.ds(TOK, MEM), :], memory_kv_ref),
            (memory_hbm, memory_ref),
        )[i]
        return pltpu.make_async_copy(source, target, rowsem.at[i])

    def main_copy(g):
        start = (g // 2) * QBLOCK + (g % 2) * MAIN
        return pltpu.make_async_copy(
            gathered.at[:, pl.ds(start, MAIN), :], wmain.at[g % SLOTS], mainsem.at[g]
        )

    def rest_copy(i):
        start = i * QBLOCK + 2 * MAIN
        return pltpu.make_async_copy(
            gathered.at[:, pl.ds(start, 2 * REST), :], wrest.at[i], restsem.at[i]
        )

    def out_copy(b):
        return pltpu.make_async_copy(
            gathered.at[:, pl.ds(OFIRST + b * OROWS, OROWS), :], out_ref.at[b], outsem.at[b]
        )

    def kv_copy(i):
        source, target = ((key_hbm, key_ref), (value_hbm, value_ref))[i % 2]
        cols = pl.ds((i // 2) * HEAD, HEAD)
        return pltpu.make_async_copy(source.at[:, cols], target.at[:, cols], kvsem.at[i])

    waiting = [rest_copy(0), main_copy(0)] + [rows_copy(i) for i in range(3, 7)]
    waiting += [main_copy(1), rest_copy(1), main_copy(2)]
    waiting += [main_copy(3)] + [out_copy(b) for b in range(CHUNKS)] + [kv_copy(i) for i in range(2 * GROUPS)]
    waiting.reverse()

    def start(count):
        for _ in range(min(count, len(waiting))):
            waiting.pop().start()

    for i in range(3):
        rows_copy(i).start()
    start(9)
    for i in range(3):
        rows_copy(i).wait()
    def attend_group(g):
        memory_kv = memory_kv_ref[g]
        q = q_ref[g, TOK:, :]
        for i in range(SETS):
            attn_ref[i, g] = attend(q, memory_kv, tokens_kv_ref[i, g], memory_kv, TOK)

    for g in range(GROUPS):
        if g % 2 == 0:
            rest_copy(g // 2).wait()
        main_copy(g).wait()
        if g == 1:
            for i in range(3, 6):
                rows_copy(i).wait()
        acc = dot(main_ref[...], wmain[g % SLOTS].reshape(DEVICES * MAIN, PAIR))
        rest_rows = (even_ref if g % 2 == 0 else odd_ref)[...]
        acc = acc + dot(rest_rows, wrest[g // 2].reshape(DEVICES * 2 * REST, PAIR))
        q_ref[g] = (acc * (1.0 / HEAD**0.5)).astype(jnp.bfloat16)
        if g > 0:
            attend_group(g - 1)
        start(3)

    def out_ready(b):
        if b == 0 or b == 4:
            for i in range(b, min(b + 4, CHUNKS)):
                out_copy(i).wait()
            start(4)

    attend_group(GROUPS - 1)
    attn = jnp.concatenate([row_blocks(attn_ref.at[i]) for i in range(SETS)], axis=0)
    total = project_out(attn, out_ref, proj_ref, out_ready)
    start(len(waiting))
    rows_copy(6).wait()
    finish_rows(proj_ref, MEM, MEM, total, memory_ref, post_ref, others_ref)

    def kv_ready(g):
        if g == 0:
            for i in range(2 * GROUPS):
                kv_copy(i).wait()

    finish_rows(proj_ref, 0, MEM, total, memory_ref, post_ref, new_ref)
    sq_ref[...] = jnp.full((8, 128), squared_change(new_ref, memory_ref), jnp.float32)
    project_read(others_ref, gain_ref, key_ref, value_ref, read_ref, kv_ready)


def middle_kernel(
    segment, previous_ref, memory_ref, squares_ref, q_ref, kv_ref, read_ref,
    gain_ref, post_ref, key_ref, value_ref, out_ref,
    new_ref, next_ref, sq_ref,
    attn_ref, proj_ref, copy_ref,
):
    for g in range(GROUPS):
        memory_kv = kv_ref[g, TOK:, :]
        own = jnp.where(segment[0] == 0, memory_kv, read_ref[g])
        attn_ref[g] = attend(q_ref[g, TOK:, :], own, kv_ref[g, :TOK, :], memory_kv, TOK)
    total = project_out(row_blocks(attn_ref), out_ref, proj_ref)
    finish_rows(proj_ref, 0, MEM, total, memory_ref, post_ref, new_ref)
    copy_ref[...] = new_ref[...]
    project_read(copy_ref, gain_ref, key_ref, value_ref, next_ref)
    lane = lax.broadcasted_iota(jnp.int32, (8, 128), 1)
    sq_ref[...] = jnp.where(lane == 0, squares_ref[...], squared_change(new_ref, previous_ref))


def last_kernel(
    segment, weight_ref, previous_ref, memory_ref, tokens_ref, squares_ref, q_ref, kv_ref,
    read_ref, post_ref, out_ref,
    tok_ref, new_ref, sq_ref,
    attn_ref, proj_ref,
):
    at_start = segment[0] == 0

    def group(g, _):
        memory_kv = kv_ref[g, TOK:, :]
        own = jnp.where(at_start, memory_kv, read_ref[g])
        attn_ref[g] = attend(q_ref[g], own, kv_ref[g, :TOK, :], memory_kv, 0)
        return 0

    lax.fori_loop(0, GROUPS, group, 0, unroll=True)
    total = project_out(row_blocks(attn_ref), out_ref, proj_ref)
    finish_rows(proj_ref, 0, TOK, total, tokens_ref, post_ref, tok_ref)
    finish_rows(proj_ref, TOK, MEM, total, memory_ref, post_ref, new_ref)
    lane = lax.broadcasted_iota(jnp.int32, (8, 128), 1)
    change = squared_change(new_ref, previous_ref)
    row = jnp.where(lane == 2, change, squares_ref[...]) * weight_ref[0]
    for i in range(DEVICES // 8):
        sq_ref[8 * i : 8 * (i + 1), :] = row


def whole():
    return pl.BlockSpec(memory_space=pltpu.VMEM)


def in_hbm():
    return pl.BlockSpec(memory_space=pltpu.HBM)


def in_smem():
    return pl.BlockSpec(memory_space=pltpu.SMEM)


def params(mib):
    return pltpu.CompilerParams(vmem_limit_bytes=mib * MIB)


def far(x):
    return pltpu.with_memory_space_constraint(x, pltpu.HBM)


def pinned(x):
    return pltpu.with_memory_space_constraint(x, pltpu.VMEM)


def pack(query_weight, output_weight):
    return pl.pallas_call(
        pack_kernel,
        name="pack",
        out_shape=jax.ShapeDtypeStruct((PACKED, PAIR), jnp.bfloat16),
        in_specs=[in_hbm(), in_hbm()],
        out_specs=whole(),
        scratch_shapes=[
            pltpu.VMEM((QROWS, GROUPS * PAIR), jnp.bfloat16),
            pltpu.VMEM((OROWS, WIDTH), jnp.bfloat16),
            pltpu.SemaphoreType.DMA,
            pltpu.SemaphoreType.DMA,
        ],
        compiler_params=params(2),
    )(far(query_weight), far(output_weight))


WRITTEN = jax.ShapeDtypeStruct((MEM, WIDTH), jnp.bfloat16)
SQUARES = jax.ShapeDtypeStruct((8, 128), jnp.float32)


def first_step(main, even, odd, memory, kv, behind, gain, post_gain, segment,
               key_matrix, value_matrix, gathered):
    near = pltpu.VMEM((WIDTH, GROUPS * HEAD), jnp.bfloat16)
    sources = (main, even, odd, memory, kv, behind)
    return pl.pallas_call(
        first_kernel,
        name="first_step",
        out_shape=(
            jax.ShapeDtypeStruct((GROUPS, ROWS, PAIR), jnp.bfloat16),
            WRITTEN,
            jax.ShapeDtypeStruct((GROUPS, MEM, PAIR), jnp.bfloat16),
            SQUARES,
            near,
            near,
            pltpu.VMEM((CHUNKS, DEVICES, OROWS, PAIR), jnp.bfloat16),
        ),
        in_specs=[in_hbm()] * 6 + [whole()] * 2 + [in_smem()] + [in_hbm()] * 3,
        out_specs=tuple(whole() for _ in range(7)),
        scratch_shapes=[pltpu.VMEM(x.shape, x.dtype) for x in sources[:4]]
        + [
            pltpu.VMEM((GROUPS, MEM, PAIR), jnp.bfloat16),
            pltpu.VMEM((SETS, GROUPS, TOK, PAIR), jnp.bfloat16),
            pltpu.VMEM((SLOTS, DEVICES, MAIN, PAIR), jnp.bfloat16),
            pltpu.VMEM((2, DEVICES, 2 * REST, PAIR), jnp.bfloat16),
            pltpu.VMEM((SETS, GROUPS, MEM, PAIR), jnp.bfloat16),
            pltpu.VMEM((CHUNKS, SETS * MEM, PAIR), jnp.float32),
            pltpu.VMEM((MEM, WIDTH), jnp.bfloat16),
            pltpu.SemaphoreType.DMA((7,)),
            pltpu.SemaphoreType.DMA((GROUPS,)),
            pltpu.SemaphoreType.DMA((2,)),
            pltpu.SemaphoreType.DMA((CHUNKS,)),
            pltpu.SemaphoreType.DMA((2 * GROUPS,)),
        ],
        compiler_params=params(20),
    )(*(far(x) for x in sources), gain, post_gain, segment, far(key_matrix), far(value_matrix),
      gathered)


def middle_step(segment, previous, memory, squares, q, kv, read, gain, post_gain,
                *weights):
    return pl.pallas_call(
        middle_kernel,
        name="middle_step",
        out_shape=(
            WRITTEN,
            jax.ShapeDtypeStruct((GROUPS, MEM, PAIR), jnp.bfloat16),
            SQUARES,
        ),
        in_specs=[in_smem()] + [whole()] * (8 + len(weights)),
        out_specs=(whole(), whole(), whole()),
        scratch_shapes=[
            pltpu.VMEM((GROUPS, MEM, PAIR), jnp.bfloat16),
            pltpu.VMEM((CHUNKS, MEM, PAIR), jnp.float32),
            pltpu.VMEM((MEM, WIDTH), jnp.bfloat16),
        ],
        compiler_params=params(5),
    )(segment, previous, memory, squares, q, kv, read, gain, post_gain,
      *(pinned(x) for x in weights))


def last_step(segment, weight, previous, memory, tokens, squares, q, kv, read, post_gain,
              out_weight):
    return pl.pallas_call(
        last_kernel,
        name="last_step",
        out_shape=(
            jax.ShapeDtypeStruct((TOK, WIDTH), jnp.bfloat16),
            WRITTEN,
            jax.ShapeDtypeStruct((DEVICES, 128), jnp.float32),
        ),
        in_specs=[in_smem(), in_smem()] + [whole()] * 9,
        out_specs=(whole(), whole(), whole()),
        scratch_shapes=[
            pltpu.VMEM((GROUPS, ROWS, PAIR), jnp.bfloat16),
            pltpu.VMEM((CHUNKS, ROWS, PAIR), jnp.float32),
        ],
        compiler_params=params(10),
    )(segment, weight, previous, memory, tokens, squares, q, kv, read, post_gain,
      pinned(out_weight))


def by_head(x):
    return jnp.transpose(x.reshape(x.shape[0], GROUPS, HEAD), (1, 0, 2))


def shards(
    tokens,
    memory,
    norm_gain,
    post_gain,
    query_weight,
    key_matrix,
    value_matrix,
    output_weight,
    segment_weight,
):
    mine = pack(query_weight, output_weight)
    gathered = lax.all_gather(mine, SEG, axis=0, tiled=False)
    inputs = jnp.concatenate([tokens, memory], axis=0)
    normed = prenorm(inputs, norm_gain)
    local_k = by_head(dot(normed, key_matrix).astype(jnp.bfloat16))
    local_v = by_head(dot(normed, value_matrix).astype(jnp.bfloat16))
    kv = jnp.concatenate([local_k, local_v], axis=2)
    tokens_kv = kv[:, :TOK, :]
    behind = from_behind(tokens_kv, SEG, 1)
    by_device = normed.reshape(ROWS, DEVICES, QROWS)
    main = by_device[:, :, :MAIN].reshape(ROWS, DEVICES * MAIN)
    rest = by_device[:, :, MAIN:]
    even = jnp.pad(rest, ((0, 0), (0, 0), (0, REST))).reshape(ROWS, DEVICES * 2 * REST)
    odd = jnp.pad(rest, ((0, 0), (0, 0), (REST, 0))).reshape(ROWS, DEVICES * 2 * REST)
    post = post_gain.reshape(1, WIDTH)
    gain = norm_gain.reshape(1, WIDTH)
    segment = lax.axis_index(SEG).astype(jnp.int32).reshape(1)
    q, newest, read, squares, near_k, near_v, near_out = first_step(
        main, even, odd, memory, kv, behind, gain, post, segment, key_matrix,
        value_matrix, gathered,
    )
    newest, read, squares = middle_step(
        segment, newest, memory, squares, q, kv, read, gain, post, near_k, near_v, near_out
    )
    read = from_behind(read, SEG, 1)
    token_out, newest, squares = last_step(
        segment, segment_weight, newest, memory, tokens, squares, q, kv, read, post, near_out
    )
    everyone = lax.all_to_all(
        squares, SEG, split_axis=0, concat_axis=0, tiled=True
    )
    totals = jnp.sum(everyone, axis=0)[:ITERS]
    change_vec = jnp.sqrt(totals / (DEVICES * MEM * WIDTH) + eps)
    return (token_out, newest, change_vec)


def solution(mesh):
    finer = Mesh(mesh.devices.reshape(4, 4, 4, 2), SEG)
    in_specs = (P(SEG, None), P(), P(), P(), P(SEG, None), P(), P(), P(SEG, None), P(SEG))
    out_specs = (P(SEG, None), P(SEG, None), P())
    return jax.shard_map(
        shards, mesh=finer, in_specs=in_specs, out_specs=out_specs, check_vma=False
    )
```

```python
import functools

import jax
import jax.numpy as jnp
from jax import lax
from jax.experimental import pallas as pl
from jax.experimental.pallas import tpu as pltpu
from jax.sharding import Mesh
from jax.sharding import PartitionSpec as P

HEAD = 256
GROUPS = 4
PAIR = 2 * HEAD
ITERS = 3
WIDTH = 3584
MEM = 64
TOK = 256
ROWS = TOK + MEM
CHUNKS = WIDTH // PAIR
QROWS = 28
MAIN = 24
REST = QROWS - MAIN
OROWS = 16
DEVICES = 128
QBLOCK = 2 * QROWS
OFIRST = GROUPS * QROWS
PACKED = OFIRST + CHUNKS * OROWS
SEG = ("seg_0", "seg_1", "seg_2", "seg_3")
MIB = 1024 * 1024

eps = 1e-06


def from_behind(block, axis, distance):
    devices = range(lax.axis_size(axis))
    route = [(i - distance, i) for i in devices if i - distance in devices]
    return lax.ppermute(block, axis, route)


def prenorm(rows, gain):
    rows = rows.astype(jnp.float32)
    mean_sq = jnp.mean(rows * rows, axis=-1, keepdims=True)
    return (rows / jnp.sqrt(mean_sq + eps) * gain).astype(jnp.bfloat16)


def dot(a, b):
    return jnp.dot(a, b, preferred_element_type=jnp.float32)


def attend(q, read, tokens, memory, row0):
    rows = q.shape[0]
    kv = jnp.concatenate([read, tokens, memory], axis=0)
    keys = kv[:, :HEAD]
    values = kv[:, HEAD:]
    both = jnp.concatenate([q[:, :HEAD], q[:, HEAD:]], axis=0)
    score = lax.dot_general(
        both, keys, (((1,), (1,)), ((), ())), preferred_element_type=jnp.float32
    )
    row = lax.broadcasted_iota(jnp.int32, score.shape, 0)
    row = jnp.where(row >= rows, row - rows, row) + row0
    col = lax.broadcasted_iota(jnp.int32, score.shape, 1)
    expo = jnp.where(col - MEM <= row, jnp.exp(score), 0.0)
    denom = jnp.sum(expo, axis=-1, keepdims=True)
    numer = dot(expo.astype(jnp.bfloat16), values)
    attn = (numer / denom).astype(jnp.bfloat16)
    return jnp.concatenate([attn[:rows], attn[rows:]], axis=1)


def row_blocks(attn_ref):
    return jnp.concatenate([attn_ref[g] for g in range(GROUPS)], axis=1)


def project_out(attn, weight_ref, proj_ref, ready=None):
    total = jnp.zeros((attn.shape[0], 1), jnp.float32)
    for b in range(CHUNKS):
        if ready is not None:
            ready(b)
        proj = dot(attn, weight_ref[b].reshape(DEVICES * OROWS, PAIR))
        proj_ref[b] = proj
        total = total + jnp.sum(proj * proj, axis=-1, keepdims=True)
    return total


def finish_rows(proj_ref, start, count, total, residual_ref, gain_ref, out_ref, at=0):
    root = jnp.sqrt(total[start : start + count] * (1.0 / WIDTH) + eps)
    for b in range(CHUNKS):
        cols = slice(b * PAIR, (b + 1) * PAIR)
        proj = proj_ref[b, start : start + count, :]
        out = residual_ref[:, cols].astype(jnp.float32) + proj / root * gain_ref[:, cols]
        out_ref[at : at + count, cols] = out.astype(jnp.bfloat16)


def squared_change(new_ref, old_ref):
    total = jnp.zeros((MEM, PAIR), jnp.float32)
    for b in range(CHUNKS):
        cols = slice(b * PAIR, (b + 1) * PAIR)
        diff = new_ref[:, cols].astype(jnp.float32) - old_ref[:, cols].astype(jnp.float32)
        total = total + diff * diff
    return jnp.sum(total)


def pack_kernel(query_hbm, output_hbm, out_ref, query_ref, output_ref, qsem, osem):
    query_copy = pltpu.make_async_copy(query_hbm, query_ref, qsem)
    output_copy = pltpu.make_async_copy(output_hbm, output_ref, osem)
    query_copy.start()
    output_copy.start()
    query_copy.wait()
    for g in range(GROUPS):
        cols = slice(g * PAIR, (g + 1) * PAIR)
        base = (g // 2) * QBLOCK
        main = base + (g % 2) * MAIN
        rest = base + 2 * MAIN + (g % 2) * REST
        out_ref[main : main + MAIN, :] = query_ref[:MAIN, cols]
        out_ref[rest : rest + REST, :] = query_ref[MAIN:, cols]
    output_copy.wait()
    for b in range(CHUNKS):
        first = OFIRST + b * OROWS
        out_ref[first : first + OROWS, :] = output_ref[:, b * PAIR : (b + 1) * PAIR]


def project_read(new_ref, gain_ref, key_ref, value_ref, kv_ref, ready=None):
    total = jnp.zeros((new_ref.shape[0], 1), jnp.float32)
    for i in range(CHUNKS):
        rows = new_ref[:, i * PAIR : (i + 1) * PAIR].astype(jnp.float32)
        total = total + jnp.sum(rows * rows, axis=-1, keepdims=True)
    root = jnp.sqrt(total * (1.0 / WIDTH) + eps)
    for i in range(CHUNKS):
        cols = slice(i * PAIR, (i + 1) * PAIR)
        rows = new_ref[:, cols].astype(jnp.float32)
        new_ref[:, cols] = (rows / root * gain_ref[:, cols]).astype(jnp.bfloat16)
    normed = new_ref[...]
    for g in range(GROUPS):
        cols = slice(g * HEAD, (g + 1) * HEAD)
        if ready is not None:
            ready(g)
        kv_ref[g, :, :HEAD] = dot(normed, key_ref[:, cols]).astype(jnp.bfloat16)
        kv_ref[g, :, HEAD:] = dot(normed, value_ref[:, cols]).astype(jnp.bfloat16)


SLOTS = 3
SETS = 2


def first_kernel(
    main_hbm, even_hbm, odd_hbm, memory_hbm, kv_hbm, behind_hbm, gain_ref, post_ref, segment,
    key_hbm, value_hbm, gathered,
    q_ref, new_ref, read_ref, sq_ref, key_ref, value_ref, out_ref,
    main_ref, even_ref, odd_ref, memory_ref, memory_kv_ref, tokens_kv_ref,
    wmain, wrest, attn_ref, proj_ref, others_ref,
    rowsem, mainsem, restsem, outsem, kvsem,
):
    def rows_copy(i):
        source, target = (
            (main_hbm, main_ref),
            (even_hbm, even_ref),
            (odd_hbm, odd_ref),
            (kv_hbm.at[:, pl.ds(0, TOK), :], tokens_kv_ref.at[0]),
            (behind_hbm, tokens_kv_ref.at[1]),
            (kv_hbm.at[:, pl.ds(TOK, MEM), :], memory_kv_ref),
            (memory_hbm, memory_ref),
        )[i]
        return pltpu.make_async_copy(source, target, rowsem.at[i])

    def main_copy(g):
        start = (g // 2) * QBLOCK + (g % 2) * MAIN
        return pltpu.make_async_copy(
            gathered.at[:, pl.ds(start, MAIN), :], wmain.at[g % SLOTS], mainsem.at[g]
        )

    def rest_copy(i):
        start = i * QBLOCK + 2 * MAIN
        return pltpu.make_async_copy(
            gathered.at[:, pl.ds(start, 2 * REST), :], wrest.at[i], restsem.at[i]
        )

    def out_copy(b):
        return pltpu.make_async_copy(
            gathered.at[:, pl.ds(OFIRST + b * OROWS, OROWS), :], out_ref.at[b], outsem.at[b]
        )

    def kv_copy(i):
        source, target = ((key_hbm, key_ref), (value_hbm, value_ref))[i % 2]
        cols = pl.ds((i // 2) * HEAD, HEAD)
        return pltpu.make_async_copy(source.at[:, cols], target.at[:, cols], kvsem.at[i])

    waiting = [rest_copy(0), main_copy(0)] + [rows_copy(i) for i in range(3, 7)]
    waiting += [main_copy(1), rest_copy(1), main_copy(2)]
    waiting += [main_copy(3)] + [out_copy(b) for b in range(CHUNKS)] + [kv_copy(i) for i in range(2 * GROUPS)]
    waiting.reverse()

    def start(count):
        for _ in range(min(count, len(waiting))):
            waiting.pop().start()

    for i in range(3):
        rows_copy(i).start()
    start(9)
    for i in range(3):
        rows_copy(i).wait()
    def attend_group(g):
        memory_kv = memory_kv_ref[g]
        q = q_ref[g, TOK:, :]
        for i in range(SETS):
            attn_ref[i, g] = attend(q, memory_kv, tokens_kv_ref[i, g], memory_kv, TOK)

    for g in range(GROUPS):
        if g % 2 == 0:
            rest_copy(g // 2).wait()
        main_copy(g).wait()
        if g == 1:
            for i in range(3, 6):
                rows_copy(i).wait()
        acc = dot(main_ref[...], wmain[g % SLOTS].reshape(DEVICES * MAIN, PAIR))
        rest_rows = (even_ref if g % 2 == 0 else odd_ref)[...]
        acc = acc + dot(rest_rows, wrest[g // 2].reshape(DEVICES * 2 * REST, PAIR))
        q_ref[g] = (acc * (1.0 / HEAD**0.5)).astype(jnp.bfloat16)
        if g > 0:
            attend_group(g - 1)
        start(3)

    def out_ready(b):
        if b == 0 or b == 4:
            for i in range(b, min(b + 4, CHUNKS)):
                out_copy(i).wait()
            start(4)

    attend_group(GROUPS - 1)
    attn = jnp.concatenate([row_blocks(attn_ref.at[i]) for i in range(SETS)], axis=0)
    total = project_out(attn, out_ref, proj_ref, out_ready)
    start(len(waiting))
    rows_copy(6).wait()
    finish_rows(proj_ref, MEM, MEM, total, memory_ref, post_ref, others_ref)

    def kv_ready(g):
        if g == 0:
            for i in range(2 * GROUPS):
                kv_copy(i).wait()

    finish_rows(proj_ref, 0, MEM, total, memory_ref, post_ref, new_ref)
    sq_ref[...] = jnp.full((8, 128), squared_change(new_ref, memory_ref), jnp.float32)
    project_read(others_ref, gain_ref, key_ref, value_ref, read_ref, kv_ready)


def middle_kernel(
    segment, previous_ref, memory_ref, squares_ref, q_ref, kv_ref, read_ref,
    gain_ref, post_ref, key_ref, value_ref, out_ref,
    new_ref, next_ref, sq_ref,
    attn_ref, proj_ref, copy_ref,
):
    for g in range(GROUPS):
        memory_kv = kv_ref[g, TOK:, :]
        own = jnp.where(segment[0] == 0, memory_kv, read_ref[g])
        attn_ref[g] = attend(q_ref[g, TOK:, :], own, kv_ref[g, :TOK, :], memory_kv, TOK)
    total = project_out(row_blocks(attn_ref), out_ref, proj_ref)
    finish_rows(proj_ref, 0, MEM, total, memory_ref, post_ref, new_ref)
    copy_ref[...] = new_ref[...]
    project_read(copy_ref, gain_ref, key_ref, value_ref, next_ref)
    lane = lax.broadcasted_iota(jnp.int32, (8, 128), 1)
    sq_ref[...] = jnp.where(lane == 0, squares_ref[...], squared_change(new_ref, previous_ref))


def last_kernel(
    segment, weight_ref, previous_ref, memory_ref, tokens_ref, squares_ref, q_ref, kv_ref,
    read_ref, post_ref, out_ref,
    tok_ref, new_ref, sq_ref,
    attn_ref, proj_ref,
):
    at_start = segment[0] == 0

    def group(g, _):
        memory_kv = kv_ref[g, TOK:, :]
        own = jnp.where(at_start, memory_kv, read_ref[g])
        attn_ref[g] = attend(q_ref[g], own, kv_ref[g, :TOK, :], memory_kv, 0)
        return 0

    lax.fori_loop(0, GROUPS, group, 0, unroll=True)
    total = project_out(row_blocks(attn_ref), out_ref, proj_ref)
    finish_rows(proj_ref, 0, TOK, total, tokens_ref, post_ref, tok_ref)
    finish_rows(proj_ref, TOK, MEM, total, memory_ref, post_ref, new_ref)
    lane = lax.broadcasted_iota(jnp.int32, (8, 128), 1)
    change = squared_change(new_ref, previous_ref)
    row = jnp.where(lane == 2, change, squares_ref[...]) * weight_ref[0]
    for i in range(DEVICES // 8):
        sq_ref[8 * i : 8 * (i + 1), :] = row


def whole():
    return pl.BlockSpec(memory_space=pltpu.VMEM)


def in_hbm():
    return pl.BlockSpec(memory_space=pltpu.HBM)


def in_smem():
    return pl.BlockSpec(memory_space=pltpu.SMEM)


def params(mib):
    return pltpu.CompilerParams(vmem_limit_bytes=mib * MIB)


def far(x):
    return pltpu.with_memory_space_constraint(x, pltpu.HBM)


def pinned(x):
    return pltpu.with_memory_space_constraint(x, pltpu.VMEM)


def pack(query_weight, output_weight):
    return pl.pallas_call(
        pack_kernel,
        name="pack",
        out_shape=jax.ShapeDtypeStruct((PACKED, PAIR), jnp.bfloat16),
        in_specs=[in_hbm(), in_hbm()],
        out_specs=whole(),
        scratch_shapes=[
            pltpu.VMEM((QROWS, GROUPS * PAIR), jnp.bfloat16),
            pltpu.VMEM((OROWS, WIDTH), jnp.bfloat16),
            pltpu.SemaphoreType.DMA,
            pltpu.SemaphoreType.DMA,
        ],
        compiler_params=params(2),
    )(far(query_weight), far(output_weight))


WRITTEN = jax.ShapeDtypeStruct((MEM, WIDTH), jnp.bfloat16)
SQUARES = jax.ShapeDtypeStruct((8, 128), jnp.float32)


def first_step(main, even, odd, memory, kv, behind, gain, post_gain, segment,
               key_matrix, value_matrix, gathered):
    near = pltpu.VMEM((WIDTH, GROUPS * HEAD), jnp.bfloat16)
    sources = (main, even, odd, memory, kv, behind)
    return pl.pallas_call(
        first_kernel,
        name="first_step",
        out_shape=(
            jax.ShapeDtypeStruct((GROUPS, ROWS, PAIR), jnp.bfloat16),
            WRITTEN,
            jax.ShapeDtypeStruct((GROUPS, MEM, PAIR), jnp.bfloat16),
            SQUARES,
            near,
            near,
            pltpu.VMEM((CHUNKS, DEVICES, OROWS, PAIR), jnp.bfloat16),
        ),
        in_specs=[in_hbm()] * 6 + [whole()] * 2 + [in_smem()] + [in_hbm()] * 3,
        out_specs=tuple(whole() for _ in range(7)),
        scratch_shapes=[pltpu.VMEM(x.shape, x.dtype) for x in sources[:4]]
        + [
            pltpu.VMEM((GROUPS, MEM, PAIR), jnp.bfloat16),
            pltpu.VMEM((SETS, GROUPS, TOK, PAIR), jnp.bfloat16),
            pltpu.VMEM((SLOTS, DEVICES, MAIN, PAIR), jnp.bfloat16),
            pltpu.VMEM((2, DEVICES, 2 * REST, PAIR), jnp.bfloat16),
            pltpu.VMEM((SETS, GROUPS, MEM, PAIR), jnp.bfloat16),
            pltpu.VMEM((CHUNKS, SETS * MEM, PAIR), jnp.float32),
            pltpu.VMEM((MEM, WIDTH), jnp.bfloat16),
            pltpu.SemaphoreType.DMA((7,)),
            pltpu.SemaphoreType.DMA((GROUPS,)),
            pltpu.SemaphoreType.DMA((2,)),
            pltpu.SemaphoreType.DMA((CHUNKS,)),
            pltpu.SemaphoreType.DMA((2 * GROUPS,)),
        ],
        compiler_params=params(20),
    )(*(far(x) for x in sources), gain, post_gain, segment, far(key_matrix), far(value_matrix),
      gathered)


def middle_step(segment, previous, memory, squares, q, kv, read, gain, post_gain,
                *weights):
    return pl.pallas_call(
        middle_kernel,
        name="middle_step",
        out_shape=(
            WRITTEN,
            jax.ShapeDtypeStruct((GROUPS, MEM, PAIR), jnp.bfloat16),
            SQUARES,
        ),
        in_specs=[in_smem()] + [whole()] * (8 + len(weights)),
        out_specs=(whole(), whole(), whole()),
        scratch_shapes=[
            pltpu.VMEM((GROUPS, MEM, PAIR), jnp.bfloat16),
            pltpu.VMEM((CHUNKS, MEM, PAIR), jnp.float32),
            pltpu.VMEM((MEM, WIDTH), jnp.bfloat16),
        ],
        compiler_params=params(5),
    )(segment, previous, memory, squares, q, kv, read, gain, post_gain,
      *(pinned(x) for x in weights))


def last_step(segment, weight, previous, memory, tokens, squares, q, kv, read, post_gain,
              out_weight):
    return pl.pallas_call(
        last_kernel,
        name="last_step",
        out_shape=(
            jax.ShapeDtypeStruct((TOK, WIDTH), jnp.bfloat16),
            WRITTEN,
            jax.ShapeDtypeStruct((DEVICES, 128), jnp.float32),
        ),
        in_specs=[in_smem(), in_smem()] + [whole()] * 9,
        out_specs=(whole(), whole(), whole()),
        scratch_shapes=[
            pltpu.VMEM((GROUPS, ROWS, PAIR), jnp.bfloat16),
            pltpu.VMEM((CHUNKS, ROWS, PAIR), jnp.float32),
        ],
        compiler_params=params(10),
    )(segment, weight, previous, memory, tokens, squares, q, kv, read, post_gain,
      pinned(out_weight))


def by_head(x):
    return jnp.transpose(x.reshape(x.shape[0], GROUPS, HEAD), (1, 0, 2))


def shards(
    tokens,
    memory,
    norm_gain,
    post_gain,
    query_weight,
    key_matrix,
    value_matrix,
    output_weight,
    segment_weight,
):
    mine = pack(query_weight, output_weight)
    gathered = lax.all_gather(mine, SEG, axis=0, tiled=False)
    inputs = jnp.concatenate([tokens, memory], axis=0)
    normed = prenorm(inputs, norm_gain)
    flat_k = dot(normed, key_matrix).astype(jnp.bfloat16)
    behind_k = from_behind(flat_k[:TOK], SEG, 1)
    flat_v = dot(normed, value_matrix).astype(jnp.bfloat16)
    behind_v = from_behind(flat_v[:TOK], SEG, 1)
    kv = jnp.concatenate([by_head(flat_k), by_head(flat_v)], axis=2)
    behind = jnp.concatenate([by_head(behind_k), by_head(behind_v)], axis=2)
    by_device = normed.reshape(ROWS, DEVICES, QROWS)
    main = by_device[:, :, :MAIN].reshape(ROWS, DEVICES * MAIN)
    rest = by_device[:, :, MAIN:]
    even = jnp.pad(rest, ((0, 0), (0, 0), (0, REST))).reshape(ROWS, DEVICES * 2 * REST)
    odd = jnp.pad(rest, ((0, 0), (0, 0), (REST, 0))).reshape(ROWS, DEVICES * 2 * REST)
    post = post_gain.reshape(1, WIDTH)
    gain = norm_gain.reshape(1, WIDTH)
    segment = lax.axis_index(SEG).astype(jnp.int32).reshape(1)
    q, newest, read, squares, near_k, near_v, near_out = first_step(
        main, even, odd, memory, kv, behind, gain, post, segment, key_matrix,
        value_matrix, gathered,
    )
    newest, read, squares = middle_step(
        segment, newest, memory, squares, q, kv, read, gain, post, near_k, near_v, near_out
    )
    read = from_behind(read, SEG, 1)
    token_out, newest, squares = last_step(
        segment, segment_weight, newest, memory, tokens, squares, q, kv, read, post, near_out
    )
    everyone = lax.all_to_all(
        squares, SEG, split_axis=0, concat_axis=0, tiled=True
    )
    totals = jnp.sum(everyone, axis=0)[:ITERS]
    change_vec = jnp.sqrt(totals / (DEVICES * MEM * WIDTH) + eps)
    return (token_out, newest, change_vec)


def solution(mesh):
    finer = Mesh(mesh.devices.reshape(4, 4, 4, 2), SEG)
    in_specs = (P(SEG, None), P(), P(), P(), P(SEG, None), P(), P(), P(SEG, None), P(SEG))
    out_specs = (P(SEG, None), P(SEG, None), P())
    return jax.shard_map(
        shards, mesh=finer, in_specs=in_specs, out_specs=out_specs, check_vma=False
    )
```
